256 devices in a mesh: worker: 16 (over y, z_lo, core), expert: 16 (over z_hi, x).
Axes of the slice: x: 4, y: 4, z: 8 (z_hi: 4, z_lo: 2; z = z_hi * 2 + z_lo), core: 2. Of those that a mesh axis runs over, the one named last changes fastest.
Arguments:
- tokens: bfloat16 [32768, 3072], P(('worker', 'expert')), may hold values from -6 to 6
- route_ids: int32 [32768, 2], P(('worker', 'expert')), may hold values from 0 to 3, as said below
- route_mix: float32 [32768, 2], P(('worker', 'expert')), may hold values from 0.1 to 1
- target: bfloat16 [32768, 3072], P(('worker', 'expert')), may hold values from -6 to 6
- step_count: int32 [16], P('worker'), may hold values from 8 to 101
- gate_weight: bfloat16 [3072, 4096], P(None, 'expert'), may hold values from -0.109375 to 0.109375
- up_weight: bfloat16 [3072, 4096], P(None, 'expert'), may hold values from -0.109375 to 0.109375
- down_weight: bfloat16 [4096, 3072], P('expert'), may hold values from -0.1875 to 0.1875
Outputs:
- outer_gate: float32 [3072, 4096], P('worker', 'expert')
- outer_up: float32 [3072, 4096], P('worker', 'expert')
- outer_down: float32 [4096, 3072], P('expert', 'worker')
- token_loss: float32 [32768], P(('worker', 'expert'))
The draws below stay inside these ranges and needn't reach their ends.
Inputs may be any that keep to these rules, and one draw needn't show every extreme that they name: `route_ids`: each token's 2 experts differ. In the 128 rows of one device no expert is named by more than 80 rows, and in every device's rows some expert is named by exactly 80.
All inputs are finite; a program needn't handle non-finite values.
Results may differ from the reference program's by a relative error of at most 0.017.
Values may be sent and summed in bfloat16 or wider, within the bound.
A program may use at most 128 MiB of HBM per device.

```python
import math
import jax
import jax.numpy as jnp
from jax import lax

D = 3072
H = 1024
EXPERTS = 4
TOPK = 2
TOK_DEV = 128
HSPLIT = 4
HD = 256
CAP = 80
TOK_WORKER = 2048
TOKENS = 32768
N_EXPERT = 16


def draw_route_ids(key, part):
    block_total = TOKENS // TOK_DEV
    others_count = EXPERTS - 1
    hot_expert = jax.random.randint(jax.random.fold_in(key, 11), (block_total,), 0, EXPERTS)
    block_keys = jax.random.split(jax.random.fold_in(key, 12), block_total)

    def one_block(block_key, hot_one):
        shuffle_key, rotation_key, swap_key = jax.random.split(block_key, 3)
        shuffle = jax.random.permutation(shuffle_key, TOK_DEV)
        rotation = jax.random.randint(rotation_key, (), 0, others_count)
        swapped = jax.random.randint(swap_key, (TOK_DEV,), 0, 2)
        rank_ids = jnp.arange(TOK_DEV)
        others = (hot_one + 1 + jnp.arange(others_count)) % EXPERTS
        cold_rank = rank_ids - CAP
        first_id = jnp.where(rank_ids < CAP, hot_one, others[(cold_rank + rotation) % others_count])
        second_id = jnp.where(rank_ids < CAP, others[(rank_ids + rotation) % others_count], others[(cold_rank + rotation + 1) % others_count])
        id_pairs = jnp.stack([first_id, second_id], axis=1)
        id_pairs = jnp.where(swapped[:, None] == 1, id_pairs[:, ::-1], id_pairs)
        return id_pairs[shuffle]
    return jax.vmap(one_block)(block_keys, hot_expert).reshape(TOKENS, TOPK).astype(jnp.int32)


def draw_step_count(key, part):
    worker_total = TOKENS // TOK_WORKER
    extra_steps = jax.random.randint(jax.random.fold_in(key, 21), (worker_total,), 0, 3 * worker_total)
    extra_steps = extra_steps.at[0].set(0).at[worker_total - 1].set(3 * worker_total)
    return (8 + 3 * jnp.arange(worker_total) + extra_steps).astype(jnp.int32)


def steps_of(key, dims, pieces, least, largest):
    level, own = 1.0, jax.random.fold_in(key, 6)
    for dim, blocks in pieces:
        steps = jnp.exp(jax.random.uniform(jax.random.fold_in(own, dim), (blocks,), jnp.float32, least / len(pieces), largest / len(pieces)))
        level = level * jnp.repeat(steps, dims[dim] // blocks).reshape([-1 if axis == dim else 1 for axis in range(len(dims))])
    return level


def gaussian(stream_key, extent, scale, most, cuts=(), dtype=jnp.bfloat16):
    result = jax.random.normal(stream_key, extent, jnp.float32) * scale
    if len(cuts) > 0:
        result = steps_of(stream_key, extent, cuts, -0.22, 0.18) * result
    return jnp.clip(result, min=-most, max=most).astype(dtype)


def setup_inputs(seed: int = 0) -> dict:
    streams_of = jax.random.split(jax.random.key(seed), 9)
    return {
        "tokens": gaussian(streams_of[0], (TOKENS, D), 1.0, 6.0, ((0, 256),)),
        "route_ids": draw_route_ids(jax.random.fold_in(streams_of[8], 71), 0),
        "route_mix": jnp.clip(jnp.exp(math.log(1.0) - 2.3025851 * jax.random.uniform(streams_of[2], (TOKENS, TOPK), jnp.float32) ** steps_of(streams_of[2], (TOKENS, TOPK), ((0, 256),), -0.2, 0.2)), 0.1, 1.0),
        "target": gaussian(streams_of[3], (TOKENS, D), 1.0, 6.0, ((0, 256),)),
        "step_count": draw_step_count(jax.random.fold_in(streams_of[8], 71), 0),
        "gate_weight": gaussian(streams_of[5], (D, EXPERTS * H), D ** -0.5, 0.109375, ((1, 16),)),
        "up_weight": gaussian(streams_of[6], (D, EXPERTS * H), D ** -0.5, 0.109375, ((1, 16),)),
        "down_weight": gaussian(streams_of[7], (EXPERTS * H, D), H ** -0.5, 0.1875, ((0, 16),)),
    }


def silu_parts(pre):
    sigmoid_val = jax.nn.sigmoid(pre)
    return pre * sigmoid_val, sigmoid_val * (1.0 + pre * (1.0 - sigmoid_val))


def contract_rows(left, right):
    return lax.dot_general(left, right, (((0,), (0,)), ((), ())), preferred_element_type=jnp.float32)


def reference(tokens, route_ids, route_mix, target, step_count, gate_weight, up_weight, down_weight):
    workers = TOKENS // TOK_WORKER
    row_limit = N_EXPERT * CAP
    tok_all = tokens.reshape(workers, TOK_WORKER, D)
    ids_all = route_ids.reshape(workers, TOK_WORKER, TOPK)
    mix_all = route_mix.reshape(workers, TOK_WORKER, TOPK)
    tgt_all = target.reshape(workers, TOK_WORKER, D)

    def one_worker(carried, inputs):
        tok_rows, worker_ids, worker_mix, worker_tgt, step_value = inputs
        weight = step_value.astype(jnp.float32)
        flat_ids = worker_ids.reshape(-1)
        flat_mix = worker_mix.reshape(-1)
        token_of = (jnp.arange(TOK_WORKER * TOPK) // TOPK).astype(jnp.int32)
        kept_state = []
        mixed_out = jnp.zeros((TOK_WORKER, D), jnp.float32)
        for expert in range(EXPERTS):
            chosen = flat_ids == expert
            ranking = (jnp.cumsum(chosen.astype(jnp.int32)) - 1).astype(jnp.int32)
            place_at = jnp.where(chosen, ranking, row_limit).astype(jnp.int32)
            row_token = jnp.zeros((row_limit,), jnp.int32).at[place_at].set(token_of, mode="drop")
            row_mix = jnp.zeros((row_limit,), jnp.float32).at[place_at].set(flat_mix.astype(jnp.float32), mode="drop")
            expert_rows = tok_rows[row_token]
            gate_pre = jnp.dot(expert_rows, gate_weight[:, expert * H:(expert + 1) * H], preferred_element_type=jnp.float32)
            up_pre = jnp.dot(expert_rows, up_weight[:, expert * H:(expert + 1) * H], preferred_element_type=jnp.float32)
            activated, slope = silu_parts(gate_pre)
            hidden = (activated * up_pre).astype(jnp.bfloat16)
            expert_out = jnp.zeros((row_limit, D), jnp.float32)
            for shard_id in range(HSPLIT):
                low = expert * H + shard_id * HD
                piece = jnp.dot(hidden[:, shard_id * HD:(shard_id + 1) * HD], down_weight[low:low + HD, :], preferred_element_type=jnp.float32).astype(jnp.bfloat16)
                expert_out = expert_out + piece.astype(jnp.float32)
            mixed_out = mixed_out.at[row_token].add(row_mix[:, None] * expert_out)
            kept_state.append((row_token, row_mix, expert_rows, gate_pre, up_pre, hidden, activated, slope))
        residual = mixed_out - worker_tgt.astype(jnp.float32)
        losses = 0.5 * jnp.mean(residual * residual, axis=1)
        sum_gate, sum_up, sum_down = carried
        for expert in range(EXPERTS):
            row_token, row_mix, expert_rows, gate_pre, up_pre, hidden, activated, slope = kept_state[expert]
            cotangent = (row_mix[:, None] * residual[row_token]).astype(jnp.bfloat16)
            down_grad = contract_rows(hidden, cotangent)
            grad_hidden = lax.dot_general(cotangent, down_weight[expert * H:(expert + 1) * H, :], (((1,), (1,)), ((), ())), preferred_element_type=jnp.float32)
            grad_gate = (grad_hidden * up_pre * slope).astype(jnp.bfloat16)
            grad_up = (grad_hidden * activated).astype(jnp.bfloat16)
            gate_grad = contract_rows(expert_rows, grad_gate)
            up_grad = contract_rows(expert_rows, grad_up)
            sum_gate = sum_gate.at[:, expert * H:(expert + 1) * H].add((weight * gate_grad).astype(jnp.bfloat16).astype(jnp.float32))
            sum_up = sum_up.at[:, expert * H:(expert + 1) * H].add((weight * up_grad).astype(jnp.bfloat16).astype(jnp.float32))
            sum_down = sum_down.at[expert * H:(expert + 1) * H, :].add((weight * down_grad).astype(jnp.bfloat16).astype(jnp.float32))
        return (sum_gate, sum_up, sum_down), losses

    initial = (jnp.zeros((D, EXPERTS * H), jnp.float32), jnp.zeros((D, EXPERTS * H), jnp.float32), jnp.zeros((EXPERTS * H, D), jnp.float32))
    sums, losses = lax.scan(one_worker, initial, (tok_all, ids_all, mix_all, tgt_all, step_count))
    total_steps = jnp.sum(step_count.astype(jnp.float32))
    return sums[0] / total_steps, sums[1] / total_steps, sums[2] / total_steps, losses.reshape(TOKENS)
```

```python
import functools

import jax
import jax.numpy as jnp
from jax import lax
from jax.experimental import pallas as pl
from jax.experimental.pallas import tpu as pltpu
from jax.sharding import PartitionSpec as P

MESH = pl.DeviceIdType.MESH
F32 = jnp.float32
BF16 = jnp.bfloat16
EXPERTS = 4
TOK = 128
D = 3072
HALF = TOK // 2
DC = 768
DB = 384


class Ids:
    def __init__(self):
        self.n = 0

    def take(self, count):
        base = self.n
        self.n += count
        return base


IDS = Ids()
T_RA, T_RB, T_LA, T_LB, T_FR, T_FL, T_C, T_CL, T_CR, T_CF = (IDS.take(1) for _ in range(10))
MT = IDS.take(8)
ST = IDS.take(16)
Z1, Z2, Z3, Z4 = (IDS.take(6) for _ in range(4))
YQ = IDS.take(24)
PX = IDS.take(4)
RX = IDS.take(24)
AG = IDS.take(40)
ZR = IDS.take(72)
YB = IDS.take(6)
YS = IDS.take(12)
FX = IDS.take(3)
N_SEM = IDS.n


def kernel(
    meta, tok, tgt, gw, uw, dw, out, loss,
    X, W1, WD, GU, H, HS, MXB, META, STEPS, R, PSD, PRV, XR, TG, G, GG, DM, ZH, ZF,
    YR1, YR2, FS, FR, LS, ssem, rsem, lsem,
):
    w = lax.axis_index("worker")
    ex = lax.axis_index("expert")
    y, zl, c = w // 4, (w // 2) % 2, w % 2
    p, x = ex // 4, ex % 4
    z = p * 2 + zl
    oc = 1 - c
    oz = 1 - zl
    xr, xl, x2 = (x + 1) % 4, (x + 3) % 4, (x + 2) % 4
    yu, yd, y2 = (y + 1) % 4, (y + 3) % 4, (y + 2) % 4
    e_out, e_in, e_opp = (p + 2 * zl + 3) % 4, (p + 5 - 2 * zl) % 4, (p + 2) % 4
    own = c * 4 + x
    right = (w, p * 4 + xr)
    left = (w, p * 4 + xl)
    core = (y * 4 + zl * 2 + oc, ex)
    z_out = (y * 4 + oz * 2 + c, e_out * 4 + x)
    z_in = (y * 4 + oz * 2 + c, ex)
    y_up = (yu * 4 + zl * 2 + c, ex)
    y_dn = (yd * 4 + zl * 2 + c, ex)
    zu, zd = (z + 1) % 8, (z + 7) % 8
    z_up = (y * 4 + (zu % 2) * 2 + c, (zu // 2) * 4 + x)
    z_dn = (y * 4 + (zd % 2) * 2 + c, (zd // 2) * 4 + x)

    def rc(i, src, dst, dev):
        return pltpu.make_async_remote_copy(
            src_ref=src, dst_ref=dst, send_sem=ssem.at[i], recv_sem=rsem.at[i],
            device_id=dev, device_id_type=MESH,
        )

    pending = []

    def send(i, src, dst, dev):
        copy = rc(i, src, dst, dev)
        copy.start()
        pending.append(copy)

    def send_later(i, src, dst, dev):
        rc(i, src, dst, dev).start()

    def arrived(i, dst):
        rc(i, dst, dst, core).wait_recv()

    def drain():
        for copy in pending:
            copy.wait_send()
        pending.clear()

    barrier = pltpu.get_barrier_semaphore()

    def greet(dev):
        pl.semaphore_signal(barrier, inc=1, device_id=dev, device_id_type=MESH)

    def slot_dev(s):
        return (y * 4 + zl * 2 + s // 4, p * 4 + s % 4)

    for i in range(1, 8):
        greet(slot_dev((own + i) % 8))
    for i in range(1, 16):
        other = (w + i) % 16
        greet((other, ex))
    greet(z_out)
    pl.semaphore_wait(barrier, 23)

    loads = [
        pltpu.make_async_copy(gw.at[:, pl.ds(c * 128, 128)], W1.at[p, 0], lsem.at[0]),
        pltpu.make_async_copy(uw.at[:, pl.ds(c * 128, 128)], W1.at[p, 1], lsem.at[1]),
        pltpu.make_async_copy(dw.at[pl.ds(c * 128, 128)], WD.at[p], lsem.at[2]),
        pltpu.make_async_copy(tok, X.at[own], lsem.at[3]),
        pltpu.make_async_copy(tgt, TG, lsem.at[4]),
        pltpu.make_async_copy(meta, META.at[own], lsem.at[5]),
        pltpu.make_async_copy(meta, STEPS.at[w], lsem.at[6]),
    ]
    for load in (loads[1], loads[2], loads[0]):
        load.start()

    A, B = pl.ds(0, HALF), pl.ds(HALF, HALF)
    send(T_RA, tok.at[A], X.at[own, A], right)
    send(T_LB, tok.at[B], X.at[own, B], left)
    send(T_RB, tok.at[B], X.at[own, B], right)
    send(T_LA, tok.at[A], X.at[own, A], left)
    send(T_C, tok, X.at[own], core)
    for load in loads[3:]:
        load.start()

    def chunk(e, k, q):
        if k == 1:
            return WD.at[e, pl.ds(32 * q, 32)]
        return W1.at[e, 1 if k == 0 else 0, pl.ds(768 * q, 768)]

    def zchunk(e, k):
        return chunk(e, k, y if k < 2 else k - 2)

    def half(e, k, q, h):
        if k == 1:
            return WD.at[e, pl.ds(32 * q + 16 * h, 16)]
        return W1.at[e, 1 if k == 0 else 0, pl.ds(768 * q + 384 * h, 384)]

    def zhalf(e, k, h):
        return half(e, k, y if k < 2 else k - 2, h)

    def z1(k):
        send(Z1 + k, zchunk(p, k), zchunk(p, k), z_out)

    def z2(k):
        arrived(Z1 + k, zchunk(e_out, k))
        send(Z2 + k, zchunk(e_out, k), zchunk(e_out, k), z_in)

    def z3(k):
        arrived(Z2 + k, zchunk(e_in, k))
        send(Z3 + k, zhalf(e_in, k, oz), zhalf(e_in, k, oz), z_out)

    def z4(k):
        arrived(Z3 + k, zhalf(e_opp, k, zl))
        send(Z4 + k, zhalf(e_opp, k, zl), zhalf(e_opp, k, zl), z_in)

    def z5(k):
        arrived(Z4 + k, zhalf(e_opp, k, oz))

    es = (e_out, e_in, e_opp)

    def yq(n, k):
        i = YQ + (n * 2 + k) * 4
        send(i, chunk(es[n], k, y), chunk(es[n], k, y), y_up)
        send(i + 1, chunk(es[n], k, y), chunk(es[n], k, y), y_dn)

    def yf(n, k):
        i = YQ + (n * 2 + k) * 4
        arrived(i, chunk(es[n], k, yd))
        send(i + 2, half(es[n], k, yd, 0), half(es[n], k, yd, 0), y_up)
        arrived(i + 1, chunk(es[n], k, yu))
        send(i + 3, half(es[n], k, yu, 1), half(es[n], k, yu, 1), y_dn)

    def ye(n, k):
        i = YQ + (n * 2 + k) * 4
        arrived(i + 2, half(es[n], k, y2, 0))
        arrived(i + 3, half(es[n], k, y2, 1))

    loads[1].wait()
    z1(0)
    loads[2].wait()
    z1(1)
    loads[0].wait()
    z1(2)

    @pl.loop(1, 8)
    def _(i):
        send_later(MT + i, meta, META.at[own], slot_dev((own + i) % 8))

    @pl.loop(1, 16)
    def _(i):
        send_later(ST + i, meta, STEPS.at[w], ((w + i) % 16, ex))

    z2(0)
    yq(0, 0)
    arrived(T_RA, X.at[c * 4 + xl, A])
    send(T_FR, X.at[c * 4 + xl, A], X.at[c * 4 + xl, A], right)
    arrived(T_LB, X.at[c * 4 + xr, B])
    send(T_FL, X.at[c * 4 + xr, B], X.at[c * 4 + xr, B], left)
    z2(1)
    yq(0, 1)
    z3(0)
    yq(1, 0)
    z1(3)
    yf(0, 0)
    z2(2)
    z3(1)
    yq(1, 1)
    z1(4)
    arrived(T_RB, X.at[c * 4 + xl, B])
    send(T_CL, X.at[c * 4 + xl], X.at[c * 4 + xl], core)
    arrived(T_LA, X.at[c * 4 + xr, A])
    send(T_CR, X.at[c * 4 + xr], X.at[c * 4 + xr], core)
    z4(0)
    z3(2)
    z1(5)
    z2(3)
    z5(0)
    yq(2, 0)
    yf(0, 1)
    yf(1, 0)
    z4(1)
    z5(1)
    yq(2, 1)
    arrived(T_FR, X.at[c * 4 + x2, A])
    arrived(T_FL, X.at[c * 4 + x2, B])
    send(T_CF, X.at[c * 4 + x2], X.at[c * 4 + x2], core)
    yf(1, 1)
    z2(4)
    z3(3)
    z4(2)
    z2(5)
    yf(2, 0)
    z3(4)
    z4(3)
    yf(2, 1)
    z3(5)
    z4(4)
    z4(5)

    for load in loads[3:]:
        load.wait()

    @pl.loop(1, 8)
    def _(i):
        arrived(MT + i, META.at[(own + 8 - i) % 8])

    @pl.loop(1, 16)
    def _(i):
        arrived(ST + i, STEPS.at[(w + 16 - i) % 16])

    lane = lax.broadcasted_iota(jnp.int32, (TOK, 128), 1)
    eye = lane == lax.broadcasted_iota(jnp.int32, (TOK, 128), 0)

    @pl.loop(0, 8)
    def _(s):
        rows = META[s]
        cols = jnp.zeros((TOK, 128), F32)
        for r in range(5):
            spread = jnp.where(eye, jnp.broadcast_to(rows[r : r + 1, :], (TOK, 128)), 0.0)
            cols = cols + jnp.where(lane == r, jnp.sum(spread, axis=1, keepdims=True), 0.0)
        MXB[s] = cols

    arrived(T_C, X.at[oc * 4 + x])
    arrived(T_CL, X.at[oc * 4 + xl])
    arrived(T_CR, X.at[oc * 4 + xr])
    arrived(T_CF, X.at[oc * 4 + x2])
    for k in range(2, 6):
        z5(k)
    for n in range(3):
        for k in range(2):
            ye(n, k)

    lane4 = lax.broadcasted_iota(jnp.int32, (512, 128), 1)

    def column(mb, r):
        rows = MXB[pl.ds(4 * mb, 4)].reshape(512, 128)
        return jnp.sum(jnp.where(lane4 == r, rows, 0.0), axis=1, keepdims=True)

    @pl.loop(0, 8)
    def _(i):
        e, mb = i // 2, i % 2
        rows = X[pl.ds(4 * mb, 4)].reshape(512, D)
        weights = jnp.concatenate([W1[e, 0], W1[e, 1]], axis=1)
        pre = jnp.dot(rows, weights, preferred_element_type=F32)
        GU[e, mb] = pre
        gate, up = pre[:, :128], pre[:, 128:]
        mixed = gate * jax.nn.sigmoid(gate) * up * column(mb, e)
        at = (pl.ds(pl.multiple_of(512 * mb, 512), 512), pl.ds(pl.multiple_of(128 * e, 128), 128))
        H[at] = mixed.astype(BF16)
        HS[at] = (mixed * column(mb, 4)).astype(BF16)

    drain()

    @pl.loop(1, 8)
    def _(i):
        rc(MT + i, meta, META.at[own], core).wait_send()

    @pl.loop(1, 16)
    def _(i):
        rc(ST + i, meta, STEPS.at[w], core).wait_send()

    G[...] = jnp.zeros_like(G)
    LS[...] = jnp.zeros_like(LS)

    def dcols(j):
        return pl.ds(pl.multiple_of(DC * j, DC), DC)

    def wd_cols(j):
        return WD[:, :, dcols(j)].reshape(512, DC)

    def hrows(who):
        return H[pl.ds(pl.multiple_of(512 * who, 512), 512), :]

    def s0(j):
        slot = j % 2

        @pl.when(j >= 2)
        def _():
            rc(PX + j - 2, PSD.at[slot], PRV.at[j - 2], core).wait_send()

        part = jnp.dot(hrows(oc), wd_cols(j), preferred_element_type=F32)
        PSD[slot] = part.astype(BF16).reshape(4, TOK, DC)
        send_later(PX + j, PSD.at[slot], PRV.at[j], core)

    def rs_copy(j, n):
        src = (
            PRV.at[j, x2, A], PRV.at[j, x2, B], PRV.at[j, xr, B], PRV.at[j, xl, A],
            PRV.at[j, xr, A], PRV.at[j, xl, B],
        )[n]
        return rc(RX + 6 * j + n, src, XR.at[j, n], right if n % 2 == 0 else left)

    def s1(j):
        arrived(PX + j, PRV.at[j])
        part = jnp.dot(hrows(c), wd_cols(j), preferred_element_type=F32)
        both = part.reshape(4, TOK, DC) + PRV[j].astype(F32)
        PRV[j] = both.astype(BF16)
        for n in range(4):
            rs_copy(j, n).start()

    def add_into(ref, other):
        ref[...] = (ref[...].astype(F32) + other[...].astype(F32)).astype(BF16)

    def s2(j):
        arrived(RX + 6 * j, XR.at[j, 0])
        add_into(PRV.at[j, xr, A], XR.at[j, 0])
        rs_copy(j, 4).start()
        arrived(RX + 6 * j + 1, XR.at[j, 1])
        add_into(PRV.at[j, xl, B], XR.at[j, 1])
        rs_copy(j, 5).start()

    def ag_copy(j, n):
        i = AG + 10 * j + n
        if n < 4:
            h = (A, B, B, A)[n]
            return rc(i, R.at[j, own, h], R.at[j, own, h], (right, left)[n % 2])
        if n == 4:
            return rc(i, R.at[j, own], R.at[j, own], core)
        if n == 5:
            return rc(i, R.at[j, c * 4 + xl, A], R.at[j, c * 4 + xl, A], right)
        if n == 6:
            return rc(i, R.at[j, c * 4 + xr, B], R.at[j, c * 4 + xr, B], left)
        s = c * 4 + (xl, xr, x2)[n - 7]
        return rc(i, R.at[j, s], R.at[j, s], core)

    def ag_arrived(j, n):
        i = AG + 10 * j + n
        near = c * 4 + (xl if n in (0, 2) else xr)
        far = oc * 4
        dst = {
            0: R.at[j, near, A], 2: R.at[j, near, B], 1: R.at[j, near, B], 3: R.at[j, near, A],
            4: R.at[j, far + x], 5: R.at[j, c * 4 + x2, A], 6: R.at[j, c * 4 + x2, B],
            7: R.at[j, far + xl], 8: R.at[j, far + xr], 9: R.at[j, far + x2],
        }[n]
        arrived(i, dst)

    def s3(j):
        for n in (2, 3, 4, 5):
            arrived(RX + 6 * j + n, XR.at[j, n])
        base = PRV[j, x].astype(F32)
        top = base[:HALF] + XR[j, 4].astype(F32) + XR[j, 3].astype(F32)
        low = base[HALF:] + XR[j, 2].astype(F32) + XR[j, 5].astype(F32)
        mixed = jnp.concatenate([top, low], axis=0)
        resid = mixed - TG[:, dcols(j)].astype(F32)
        square = resid * resid
        folded = square[:, :128]
        for n in range(1, 6):
            folded = folded + square[:, 128 * n : 128 * (n + 1)]
        LS[...] += folded
        R[j, own] = resid.astype(BF16)
        for n in (0, 1, 2, 3, 4):
            ag_copy(j, n).start()

    def s4(j):
        ag_arrived(j, 0)
        ag_copy(j, 5).start()
        ag_arrived(j, 1)
        ag_copy(j, 6).start()
        ag_arrived(j, 2)
        ag_copy(j, 7).start()
        ag_arrived(j, 3)
        ag_copy(j, 8).start()

    def s5(j):
        ag_arrived(j, 5)
        ag_arrived(j, 6)
        ag_copy(j, 9).start()

    def piece(m, j, dest):
        return DM.at[m, dest // 2, j, dest % 2]

    def z_copy(q, m, j, step, way):
        i = ZR + 8 * q + 2 * step + way
        dest = (z + (4 - step if way == 0 else 4 + step)) % 8
        dev = z_up if way == 0 else z_dn
        if step == 0:
            return rc(i, piece(m, j, dest).at[A if way == 0 else B], ZH.at[q, way], dev)
        return rc(i, piece(m, j, dest), ZF.at[q, way, step - 1], dev)

    def z_start(q, m, j):
        z_copy(q, m, j, 0, 0).start()
        z_copy(q, m, j, 0, 1).start()

    def z_step(q, m, j, step):
        for way in range(2):
            i = ZR + 8 * q + 2 * (step - 1) + way
            dest = (z + (4 - step if way == 0 else 4 + step)) % 8
            if step == 1:
                arrived(i, ZH.at[q, way])
                add_into(piece(m, j, dest).at[A if way == 0 else B], ZH.at[q, way])
            else:
                arrived(i, ZF.at[q, way, step - 2])
                add_into(piece(m, j, dest), ZF.at[q, way, step - 2])
            z_copy(q, m, j, step, way).start()

    def z_sum(q, m, j):
        for way in range(2):
            arrived(ZR + 8 * q + 6 + way, ZF.at[q, way, 2])
        mine = piece(m, j, z)[...].astype(F32)
        return mine + ZF[q, 0, 2].astype(F32) + ZF[q, 1, 2].astype(F32)

    def z_end(q, m, j):
        total = z_sum(q, m, j)
        DM[m, p, j, zl] = total.astype(BF16)

    def z_drain(q, m, j):
        for step in range(4):
            for way in range(2):
                z_copy(q, m, j, step, way).wait_send()

    def s6(j):
        for n in (4, 7, 8, 9):
            ag_arrived(j, n)
        rows = R[j].reshape(1024, DC)
        down = lax.dot_general(HS[...], rows, (((0,), (0,)), ((), ())), preferred_element_type=F32)
        for e in range(4):
            for b in range(2):
                DM[2, e, j, b] = down[128 * e : 128 * (e + 1), DB * b : DB * (b + 1)].astype(BF16)
        z_start(j, 2, j)
        G[...] += lax.dot_general(
            rows, wd_cols(j), (((1,), (1,)), ((), ())), preferred_element_type=F32
        )

    stages = [s1, s2, s3, s4, s5, s6] + [
        functools.partial(lambda j, step: z_step(j, 2, j, step), step=step) for step in (1, 2, 3)
    ]

    @pl.loop(0, 10)
    def _(t):
        @pl.when(t < 4)
        def _():
            s0(t)

        for n, stage in enumerate(stages):
            j = t - (n + 1)

            @pl.when((j >= 0) & (j < 4))
            def _():
                stage(j)

    mean = jnp.sum(LS[...], axis=1, keepdims=True) * (0.5 / D)
    loss[...] = jnp.sum(jnp.where(eye, mean, 0.0), axis=0, keepdims=True)

    @pl.loop(0, 8)
    def _(i):
        e, mb = i // 2, i % 2
        at = (pl.ds(pl.multiple_of(512 * mb, 512), 512), pl.ds(pl.multiple_of(128 * e, 128), 128))
        grad = G[at] * (column(mb, e) * column(mb, 4))
        pre = GU[e, mb]
        gate, up = pre[:, :128], pre[:, 128:]
        sig = jax.nn.sigmoid(gate)
        rows = at[0]
        GG[rows, pl.ds(pl.multiple_of(256 * e, 128), 128)] = (
            grad * up * (sig * (1.0 + gate * (1.0 - sig)))
        ).astype(BF16)
        GG[rows, pl.ds(pl.multiple_of(256 * e + 128, 128), 128)] = (grad * (gate * sig)).astype(BF16)

    def dw_chunk(j):
        rows = X[:, :, dcols(j)].reshape(1024, DC)

        @pl.loop(0, 4)
        def _(e):
            left_rows = GG[:, pl.ds(pl.multiple_of(256 * e, 256), 256)]
            grads = lax.dot_general(left_rows, rows, (((0,), (0,)), ((), ())), preferred_element_type=F32)
            for m in range(2):
                for b in range(2):
                    DM[m, e, j, b] = grads[128 * m : 128 * (m + 1), DB * b : DB * (b + 1)].astype(BF16)

    lo, hi = pl.ds(0, 2), pl.ds(2, 2)

    def yb_copy(n):
        src = (
            DM.at[0, lo, y2], DM.at[0, hi, y2], DM.at[0, hi, yu], DM.at[0, lo, yd],
            DM.at[0, lo, yu], DM.at[0, hi, yd],
        )[n]
        return rc(YB + n, src, YR1.at[n], y_up if n % 2 == 0 else y_dn)

    def ys_copy(m, n):
        src = (
            DM.at[m, p, y2, zl, A], DM.at[m, p, y2, zl, B], DM.at[m, p, yu, zl, B],
            DM.at[m, p, yd, zl, A], DM.at[m, p, yu, zl, A], DM.at[m, p, yd, zl, B],
        )[n]
        return rc(YS + 6 * (m - 1) + n, src, YR2.at[m - 1, n], y_up if n % 2 == 0 else y_dn)

    def yb_add(n, ref):
        arrived(YB + n, YR1.at[n])
        for a in range(2):
            for b in range(2):
                add_into(ref.at[a, b], YR1.at[n, a, b])

    def ys_start(m):
        for n in range(4):
            ys_copy(m, n).start()

    def ys_step(m):
        arrived(YS + 6 * (m - 1), YR2.at[m - 1, 0])
        add_into(DM.at[m, p, yu, zl, A], YR2.at[m - 1, 0])
        ys_copy(m, 4).start()
        arrived(YS + 6 * (m - 1) + 1, YR2.at[m - 1, 1])
        add_into(DM.at[m, p, yd, zl, B], YR2.at[m - 1, 1])
        ys_copy(m, 5).start()

    def ys_sum(m):
        for n in range(2, 6):
            arrived(YS + 6 * (m - 1) + n, YR2.at[m - 1, n])
        mine = DM[m, p, y, zl].astype(F32)
        top = mine[:HALF] + YR2[m - 1, 4].astype(F32) + YR2[m - 1, 3].astype(F32)
        low = mine[HALF:] + YR2[m - 1, 2].astype(F32) + YR2[m - 1, 5].astype(F32)
        return jnp.concatenate([top, low], axis=0)

    total_steps = jnp.sum(STEPS[...], axis=0)[4:5, :]
    mine_rows = pl.ds(pl.multiple_of(192 * c, 192), 192)
    other_rows = pl.ds(pl.multiple_of(192 * oc, 192), 192)

    def finish(m, total):
        FS[m] = total.T / total_steps
        rc(FX + m, FS.at[m, other_rows], FR.at[m], core).start()

    def up_step(n, step):
        j = (y2, yu, yd, y)[n]
        if step == 0:
            z_start(4 + n, 1, j)
        elif step < 4:
            z_step(4 + n, 1, j, step)
        else:
            z_end(4 + n, 1, j)

    z_step(1, 2, 1, 3)
    z_step(2, 2, 2, 2)
    z_step(3, 2, 3, 1)
    dw_chunk(y2)
    yb_copy(0).start()
    yb_copy(1).start()
    up_step(0, 0)
    z_end(0, 2, 0)
    z_step(2, 2, 2, 3)
    z_step(3, 2, 3, 2)
    dw_chunk(yu)
    yb_copy(2).start()
    up_step(1, 0)
    z_end(1, 2, 1)
    z_step(3, 2, 3, 3)
    dw_chunk(yd)
    yb_copy(3).start()
    up_step(2, 0)
    up_step(0, 1)
    dw_chunk(y)
    up_step(3, 0)
    yb_add(0, DM.at[0, lo, yu])
    yb_copy(4).start()
    yb_add(1, DM.at[0, hi, yd])
    yb_copy(5).start()
    z_end(2, 2, 2)
    z_end(3, 2, 3)
    ys_start(2)
    up_step(1, 1)
    up_step(0, 2)
    up_step(2, 1)
    up_step(1, 2)
    up_step(0, 3)
    up_step(3, 1)
    ys_step(2)
    up_step(2, 2)
    up_step(1, 3)
    up_step(0, 4)
    up_step(3, 2)
    up_step(2, 3)
    up_step(1, 4)
    up_step(3, 3)
    finish(2, ys_sum(2))
    yb_add(3, DM.at[0, lo, y])
    yb_add(4, DM.at[0, lo, y])
    yb_add(2, DM.at[0, hi, y])
    yb_add(5, DM.at[0, hi, y])
    z_start(8, 0, y)
    up_step(2, 4)
    up_step(3, 4)
    ys_start(1)
    z_step(8, 0, y, 1)
    ys_step(1)
    z_step(8, 0, y, 2)
    finish(1, ys_sum(1))
    z_step(8, 0, y, 3)
    finish(0, z_sum(8, 0, y))

    lanes = pl.ds(pl.multiple_of(128 * c, 128), 128)
    other_lanes = pl.ds(pl.multiple_of(128 * oc, 128), 128)
    for m in (2, 1, 0):
        out[m, :, lanes] = FS[m, mine_rows]
        arrived(FX + m, FR.at[m])
        out[m, :, other_lanes] = FR[m]

    @pl.loop(0, 4)
    def _(j):
        @pl.when(j >= 2)
        def _():
            rc(PX + j, PSD.at[j % 2], PRV.at[j], core).wait_send()

        for n in range(6):
            rs_copy(j, n).wait_send()
        for n in range(10):
            ag_copy(j, n).wait_send()
        z_drain(j, 2, j)

    for n in range(4):
        z_drain(4 + n, 1, (y2, yu, yd, y)[n])
    z_drain(8, 0, y)
    for n in range(6):
        yb_copy(n).wait_send()
        ys_copy(1, n).wait_send()
        ys_copy(2, n).wait_send()
    for m in range(3):
        rc(FX + m, FS.at[m, other_rows], FR.at[m], core).wait_send()


def per_device(tokens, route_ids, route_mix, target, step_count, gate_weight, up_weight, down_weight):
    experts = jnp.arange(EXPERTS, dtype=jnp.int32)[:, None, None]
    mix = jnp.sum(jnp.where(route_ids[None] == experts, route_mix[None], 0.0), axis=2)
    step = jnp.broadcast_to(step_count.astype(F32)[:, None], (1, TOK))
    meta = jnp.concatenate([mix, step, jnp.zeros((3, TOK), F32)], axis=0)
    any_spec = pl.BlockSpec(memory_space=pl.ANY)
    vmem_spec = pl.BlockSpec(memory_space=pltpu.VMEM)
    out, loss = pl.pallas_call(
        kernel,
        out_shape=(
            jax.ShapeDtypeStruct((3, 192, 256), F32),
            jax.ShapeDtypeStruct((1, TOK), F32),
        ),
        in_specs=[any_spec] * 6,
        out_specs=(vmem_spec, vmem_spec),
        scratch_shapes=[
            pltpu.VMEM((8, TOK, D), BF16),
            pltpu.VMEM((4, 2, D, 128), BF16),
            pltpu.VMEM((4, 128, D), BF16),
            pltpu.VMEM((4, 2, 512, 256), F32),
            pltpu.VMEM((1024, 512), BF16),
            pltpu.VMEM((1024, 512), BF16),
            pltpu.VMEM((8, TOK, 128), F32),
            pltpu.VMEM((8, 8, 128), F32),
            pltpu.VMEM((16, 8, 128), F32),
            pltpu.VMEM((4, 8, TOK, DC), BF16),
            pltpu.VMEM((2, 4, TOK, DC), BF16),
            pltpu.VMEM((4, 4, TOK, DC), BF16),
            pltpu.VMEM((4, 6, HALF, DC), BF16),
            pltpu.VMEM((TOK, D), BF16),
            pltpu.VMEM((1024, 512), F32),
            pltpu.VMEM((1024, 1024), BF16),
            pltpu.VMEM((3, 4, 4, 2, 128, DB), BF16),
            pltpu.VMEM((9, 2, HALF, DB), BF16),
            pltpu.VMEM((9, 2, 3, 128, DB), BF16),
            pltpu.VMEM((6, 2, 2, 128, DB), BF16),
            pltpu.VMEM((2, 6, HALF, DB), BF16),
            pltpu.VMEM((3, DB, 128), F32),
            pltpu.VMEM((3, 192, 128), F32),
            pltpu.VMEM((TOK, 128), F32),
            pltpu.SemaphoreType.DMA((N_SEM,)),
            pltpu.SemaphoreType.DMA((N_SEM,)),
            pltpu.SemaphoreType.DMA((7,)),
        ],
        compiler_params=pltpu.CompilerParams(
            collective_id=0, has_side_effects=True, vmem_limit_bytes=67043328
        ),
    )(meta, tokens, target, gate_weight, up_weight, down_weight)
    return out[0], out[1], out[2].T, loss.reshape(TOK)


def solution(mesh):
    return jax.shard_map(
        per_device,
        mesh=mesh,
        in_specs=(
            P(("worker", "expert"), None),
            P(("worker", "expert"), None),
            P(("worker", "expert"), None),
            P(("worker", "expert"), None),
            P("worker"),
            P(None, "expert"),
            P(None, "expert"),
            P("expert", None),
        ),
        out_specs=(
            P("worker", "expert"),
            P("worker", "expert"),
            P("expert", "worker"),
            P(("worker", "expert")),
        ),
        check_vma=False,
    )
```

```python
import functools

import jax
import jax.numpy as jnp
from jax import lax
from jax.experimental import pallas as pl
from jax.experimental.pallas import tpu as pltpu
from jax.sharding import PartitionSpec as P

MESH = pl.DeviceIdType.MESH
F32 = jnp.float32
BF16 = jnp.bfloat16
EXPERTS = 4
TOK = 128
D = 3072
HALF = TOK // 2
DC = 768
DB = 384


class Ids:
    def __init__(self):
        self.n = 0

    def take(self, count):
        base = self.n
        self.n += count
        return base


IDS = Ids()
T_RA, T_RB, T_LA, T_LB, T_FR, T_FL, T_C, T_CL, T_CR, T_CF = (IDS.take(1) for _ in range(10))
MS = IDS.take(1)
Z1, Z2, Z3, Z4 = (IDS.take(9) for _ in range(4))
YQ = IDS.take(36)
PX = IDS.take(4)
RX = IDS.take(24)
AG = IDS.take(40)
ZR = IDS.take(72)
YB = IDS.take(6)
YS = IDS.take(6)
FX = IDS.take(3)
N_SEM = IDS.n
S_TOK, S_W, S_META, S_RX, S_AG, S_YB, S_YS, S_PX, S_ZR, N_SEND = 0, 1, 2, 3, 4, 5, 6, 8, 12, 21
S_FX = N_SEND
N_SEND += 3


def kernel(
    meta, tok, tgt, gw, uw, dw, out,
    X, W1, WD, GU, H, HS, MXB, META, STEPS, R, PSD, PRV, XR, TG, G, GG, DM, ZH, ZF,
    YR1, YR2, FS, FR, LS, ssem, rsem, lsem,
):
    w = lax.axis_index("worker")
    ex = lax.axis_index("expert")
    y, zl, c = w // 4, (w // 2) % 2, w % 2
    p, x = ex // 4, ex % 4
    z = p * 2 + zl
    oc = 1 - c
    oz = 1 - zl
    xr, xl, x2 = (x + 1) % 4, (x + 3) % 4, (x + 2) % 4
    yu, yd, y2 = (y + 1) % 4, (y + 3) % 4, (y + 2) % 4
    e_out, e_in, e_opp = (p + 2 * zl + 3) % 4, (p + 5 - 2 * zl) % 4, (p + 2) % 4
    own = c * 4 + x
    right = (w, p * 4 + xr)
    left = (w, p * 4 + xl)
    core = (y * 4 + zl * 2 + oc, ex)
    z_out = (y * 4 + oz * 2 + c, e_out * 4 + x)
    z_in = (y * 4 + oz * 2 + c, ex)
    y_up = (yu * 4 + zl * 2 + c, ex)
    y_dn = (yd * 4 + zl * 2 + c, ex)
    zu, zd = (z + 1) % 8, (z + 7) % 8
    z_up = (y * 4 + (zu % 2) * 2 + c, (zu // 2) * 4 + x)
    z_dn = (y * 4 + (zd % 2) * 2 + c, (zd // 2) * 4 + x)

    def rc(i, src, dst, dev, group=0):
        return pltpu.make_async_remote_copy(
            src_ref=src, dst_ref=dst, send_sem=ssem.at[group], recv_sem=rsem.at[i],
            device_id=dev, device_id_type=MESH,
        )

    def send(i, src, dst, dev):
        rc(i, src, dst, dev, S_TOK if i < MS else S_W).start()

    def sent(group, ref):
        rc(0, ref, ref, core, group).wait_send()

    def arrived(i, dst):
        rc(i, dst, dst, core).wait_recv()

    loads = [
        pltpu.make_async_copy(gw.at[:, pl.ds(c * 128, 128)], W1.at[p, 0], lsem.at[0]),
        pltpu.make_async_copy(uw.at[:, pl.ds(c * 128, 128)], W1.at[p, 1], lsem.at[1]),
        pltpu.make_async_copy(dw.at[pl.ds(c * 128, 128)], WD.at[p], lsem.at[2]),
        pltpu.make_async_copy(tok, X.at[own], lsem.at[3]),
        pltpu.make_async_copy(tgt, TG, lsem.at[4]),
        pltpu.make_async_copy(meta, META.at[own], lsem.at[5]),
        pltpu.make_async_copy(meta, STEPS.at[w], lsem.at[6]),
    ]
    for load in (loads[1], loads[0], loads[2], *loads[3:]):
        load.start()

    barrier = pltpu.get_barrier_semaphore()

    def greet(dev):
        pl.semaphore_signal(barrier, inc=1, device_id=dev, device_id_type=MESH)

    def slot_dev(s):
        return (y * 4 + zl * 2 + s // 4, p * 4 + s % 4)

    for i in range(1, 8):
        greet(slot_dev((own + i) % 8))
    for i in range(1, 16):
        other = (w + i) % 16
        greet((other, ex))
    greet(z_out)
    pl.semaphore_wait(barrier, 23)

    A, B = pl.ds(0, HALF), pl.ds(HALF, HALF)
    send(T_RA, tok.at[A], X.at[own, A], right)
    send(T_LB, tok.at[B], X.at[own, B], left)
    send(T_RB, tok.at[B], X.at[own, B], right)
    send(T_LA, tok.at[A], X.at[own, A], left)
    send(T_C, tok, X.at[own], core)

    quarter = {0: 768, 1: 256, 6: 32}
    along_y = (0, 1, 6)

    def rows_of(e, k, first, count):
        if k == 0:
            return W1.at[e, 1, pl.ds(first, count)]
        if k == 1:
            return W1.at[e, 0, pl.ds(2048 + first, count)]
        if k < 6:
            return W1.at[e, 0, pl.ds(512 * (k - 2) + first, count)]
        if k == 6:
            return WD.at[e, pl.ds(first, count), pl.ds(0, 1536)]
        return WD.at[e, pl.ds(first, count), pl.ds(1536 + 768 * (k - 7), 768)]

    def chunk(e, k, q):
        return rows_of(e, k, quarter[k] * q, quarter[k])

    def half(e, k, q, h):
        n = quarter[k] // 2
        return rows_of(e, k, quarter[k] * q + n * h, n)

    def zchunk(e, k):
        if k in quarter:
            return chunk(e, k, y)
        return rows_of(e, k, 0, 512 if k < 6 else 128)

    def zhalf(e, k, h):
        if k in quarter:
            return half(e, k, y, h)
        n = 256 if k < 6 else 64
        return rows_of(e, k, n * h, n)

    def z1(k):
        send(Z1 + k, zchunk(p, k), zchunk(p, k), z_out)

    def z2(k):
        arrived(Z1 + k, zchunk(e_out, k))
        send(Z2 + k, zchunk(e_out, k), zchunk(e_out, k), z_in)

    def z3(k):
        arrived(Z2 + k, zchunk(e_in, k))
        send(Z3 + k, zhalf(e_in, k, oz), zhalf(e_in, k, oz), z_out)

    def z4(k):
        arrived(Z3 + k, zhalf(e_opp, k, zl))
        send(Z4 + k, zhalf(e_opp, k, zl), zhalf(e_opp, k, zl), z_in)

    def z5(k):
        arrived(Z4 + k, zhalf(e_opp, k, oz))

    es = (e_out, e_in, e_opp)

    def yid(n, k):
        return YQ + (n * 3 + along_y.index(k)) * 4

    def yq(n, k):
        i = yid(n, k)
        send(i, chunk(es[n], k, y), chunk(es[n], k, y), y_up)
        send(i + 1, chunk(es[n], k, y), chunk(es[n], k, y), y_dn)

    def yf(n, k):
        i = yid(n, k)
        arrived(i, chunk(es[n], k, yd))
        send(i + 2, half(es[n], k, yd, 0), half(es[n], k, yd, 0), y_up)
        arrived(i + 1, chunk(es[n], k, yu))
        send(i + 3, half(es[n], k, yu, 1), half(es[n], k, yu, 1), y_dn)

    def ye(n, k):
        i = yid(n, k)
        arrived(i + 2, half(es[n], k, y2, 0))
        arrived(i + 3, half(es[n], k, y2, 1))

    lane4 = lax.broadcasted_iota(jnp.int32, (512, 128), 1)

    def column(mb, r):
        rows = MXB[pl.ds(4 * mb, 4)].reshape(512, 128)
        return jnp.sum(jnp.where(lane4 == r, rows, 0.0), axis=1, keepdims=True)

    def forward(e):
        @pl.loop(0, 2)
        def _(mb):
            rows = X[pl.ds(4 * mb, 4)].reshape(512, D)
            weights = jnp.concatenate([W1[e, 0], W1[e, 1]], axis=1)
            pre = jnp.dot(rows, weights, preferred_element_type=F32)
            GU[e, mb] = pre
            gate, up = pre[:, :128], pre[:, 128:]
            mixed = gate * jax.nn.sigmoid(gate) * up * column(mb, e)
            at = (
                pl.ds(pl.multiple_of(512 * mb, 512), 512),
                pl.ds(pl.multiple_of(128 * e, 128), 128),
            )
            H[at] = mixed.astype(BF16)
            HS[at] = (mixed * column(mb, 4)).astype(BF16)

    loads[1].wait()
    z1(0)
    loads[0].wait()
    z1(1)
    z1(2)
    z1(3)
    loads[2].wait()

    @pl.loop(1, 8)
    def _(i):
        rc(MS, meta, META.at[own], slot_dev((own + i) % 8), S_META).start()

    @pl.loop(1, 16)
    def _(i):
        rc(MS, meta, STEPS.at[w], ((w + i) % 16, ex), S_META).start()

    z2(0)
    yq(0, 0)
    z2(1)
    yq(0, 1)
    arrived(T_RA, X.at[c * 4 + xl, A])
    send(T_FR, X.at[c * 4 + xl, A], X.at[c * 4 + xl, A], right)
    arrived(T_LB, X.at[c * 4 + xr, B])
    send(T_FL, X.at[c * 4 + xr, B], X.at[c * 4 + xr, B], left)
    z2(2)
    z3(0)
    yq(1, 0)
    z3(1)
    yq(1, 1)
    z1(4)
    z1(5)
    z2(3)
    yf(0, 0)
    z3(2)
    z4(0)
    yf(0, 1)
    z4(1)
    z3(3)
    z1(6)
    arrived(T_RB, X.at[c * 4 + xl, B])
    send(T_CL, X.at[c * 4 + xl], X.at[c * 4 + xl], core)
    arrived(T_LA, X.at[c * 4 + xr, A])
    send(T_CR, X.at[c * 4 + xr], X.at[c * 4 + xr], core)
    z5(0)
    yq(2, 0)
    z5(1)
    yq(2, 1)
    z2(4)
    yf(1, 0)
    z2(5)
    z4(2)
    z3(4)
    yf(1, 1)
    z4(3)
    z3(5)
    z2(6)
    yq(0, 6)
    arrived(T_FR, X.at[c * 4 + x2, A])
    arrived(T_FL, X.at[c * 4 + x2, B])
    send(T_CF, X.at[c * 4 + x2], X.at[c * 4 + x2], core)

    for load in loads[3:]:
        load.wait()

    arrived(MS, FS.at[0, pl.ds(0, 8 * 22)])

    lane = lax.broadcasted_iota(jnp.int32, (TOK, 128), 1)
    eye = lane == lax.broadcasted_iota(jnp.int32, (TOK, 128), 0)

    @pl.loop(0, 8)
    def _(s):
        rows = META[s]
        cols = jnp.zeros((TOK, 128), F32)
        for r in range(5):
            spread = jnp.where(eye, jnp.broadcast_to(rows[r : r + 1, :], (TOK, 128)), 0.0)
            cols = cols + jnp.where(lane == r, jnp.sum(spread, axis=1, keepdims=True), 0.0)
        MXB[s] = cols

    z3(6)
    yq(1, 6)
    z1(7)
    z1(8)
    arrived(T_C, X.at[oc * 4 + x])
    arrived(T_CL, X.at[oc * 4 + xl])
    arrived(T_CR, X.at[oc * 4 + xr])
    arrived(T_CF, X.at[oc * 4 + x2])
    forward(p)
    yf(2, 0)
    z4(4)
    z4(5)
    z4(6)
    z5(6)
    yq(2, 6)
    yf(2, 1)
    ye(0, 0)
    ye(0, 1)
    forward(e_out)
    yf(0, 6)
    ye(1, 0)
    ye(1, 1)
    forward(e_in)
    yf(1, 6)
    for k in range(2, 6):
        z5(k)
    ye(2, 0)
    ye(2, 1)
    forward(e_opp)
    yf(2, 6)
    z2(7)
    for n in range(3):
        ye(n, 6)

    G[...] = jnp.zeros_like(G)
    LS[...] = jnp.zeros_like(LS)

    def dcols(j):
        return pl.ds(pl.multiple_of(DC * j, DC), DC)

    def wd_cols(j):
        return WD[:, :, dcols(j)].reshape(512, DC)

    def hrows(who):
        return H[pl.ds(pl.multiple_of(512 * who, 512), 512), :]

    def s0(j):
        slot = j % 2

        @pl.when(j >= 2)
        def _():
            sent(S_PX + j - 2, PSD.at[slot])

        part = jnp.dot(hrows(oc), wd_cols(j), preferred_element_type=F32)
        PSD[slot] = part.astype(BF16).reshape(4, TOK, DC)
        rc(PX + j, PSD.at[slot], PRV.at[j], core, S_PX + j).start()

    def rs_copy(j, n):
        src = (
            PRV.at[j, x2, A], PRV.at[j, x2, B], PRV.at[j, xr, B], PRV.at[j, xl, A],
            PRV.at[j, xr, A], PRV.at[j, xl, B],
        )[n]
        return rc(RX + 6 * j + n, src, XR.at[j, n], right if n % 2 == 0 else left, S_RX)

    def s1(j):
        arrived(PX + j, PRV.at[j])
        part = jnp.dot(hrows(c), wd_cols(j), preferred_element_type=F32)
        both = part.reshape(4, TOK, DC) + PRV[j].astype(F32)
        PRV[j] = both.astype(BF16)
        for n in range(4):
            rs_copy(j, n).start()

    def add_into(ref, other):
        ref[...] = ref[...] + other[...]

    def s2(j):
        arrived(RX + 6 * j, XR.at[j, 0])
        add_into(PRV.at[j, xr, A], XR.at[j, 0])
        rs_copy(j, 4).start()
        arrived(RX + 6 * j + 1, XR.at[j, 1])
        add_into(PRV.at[j, xl, B], XR.at[j, 1])
        rs_copy(j, 5).start()

    def ag_copy(j, n):
        i = AG + 10 * j + n
        if n < 4:
            h = (A, B, B, A)[n]
            return rc(i, R.at[j, own, h], R.at[j, own, h], (right, left)[n % 2], S_AG)
        if n == 4:
            return rc(i, R.at[j, own], R.at[j, own], core, S_AG)
        if n == 5:
            return rc(i, R.at[j, c * 4 + xl, A], R.at[j, c * 4 + xl, A], right, S_AG)
        if n == 6:
            return rc(i, R.at[j, c * 4 + xr, B], R.at[j, c * 4 + xr, B], left, S_AG)
        s = c * 4 + (xl, xr, x2)[n - 7]
        return rc(i, R.at[j, s], R.at[j, s], core, S_AG)

    def ag_arrived(j, n):
        i = AG + 10 * j + n
        near = c * 4 + (xl if n in (0, 2) else xr)
        far = oc * 4
        dst = {
            0: R.at[j, near, A], 2: R.at[j, near, B], 1: R.at[j, near, B], 3: R.at[j, near, A],
            4: R.at[j, far + x], 5: R.at[j, c * 4 + x2, A], 6: R.at[j, c * 4 + x2, B],
            7: R.at[j, far + xl], 8: R.at[j, far + xr], 9: R.at[j, far + x2],
        }[n]
        arrived(i, dst)

    def s3(j):
        for n in (2, 3, 4, 5):
            arrived(RX + 6 * j + n, XR.at[j, n])
        base = PRV[j, x].astype(F32)
        top = base[:HALF] + XR[j, 4].astype(F32) + XR[j, 3].astype(F32)
        low = base[HALF:] + XR[j, 2].astype(F32) + XR[j, 5].astype(F32)
        mixed = jnp.concatenate([top, low], axis=0)
        resid = mixed - TG[:, dcols(j)].astype(F32)
        square = resid * resid
        folded = square[:, :128]
        for n in range(1, 6):
            folded = folded + square[:, 128 * n : 128 * (n + 1)]
        LS[...] += folded
        R[j, own] = resid.astype(BF16)
        for n in (0, 1, 2, 3, 4):
            ag_copy(j, n).start()

    def s4(j):
        ag_arrived(j, 0)
        ag_copy(j, 5).start()
        ag_arrived(j, 1)
        ag_copy(j, 6).start()
        ag_arrived(j, 2)
        ag_copy(j, 7).start()
        ag_arrived(j, 3)
        ag_copy(j, 8).start()

    def s5(j):
        ag_arrived(j, 5)
        ag_arrived(j, 6)
        ag_copy(j, 9).start()

    def piece(m, j, dest):
        return DM.at[m, dest // 2, j, dest % 2]

    def z_copy(q, m, j, step, way):
        i = ZR + 8 * q + 2 * step + way
        dest = (z + (4 - step if way == 0 else 4 + step)) % 8
        dev = z_up if way == 0 else z_dn
        if step == 0:
            return rc(i, piece(m, j, dest).at[A if way == 0 else B], ZH.at[q, way], dev, S_ZR + q)
        return rc(i, piece(m, j, dest), ZF.at[q, way, step - 1], dev, S_ZR + q)

    def z_start(q, m, j):
        z_copy(q, m, j, 0, 0).start()
        z_copy(q, m, j, 0, 1).start()

    def z_step(q, m, j, step):
        for way in range(2):
            i = ZR + 8 * q + 2 * (step - 1) + way
            dest = (z + (4 - step if way == 0 else 4 + step)) % 8
            if step == 1:
                arrived(i, ZH.at[q, way])
                add_into(piece(m, j, dest).at[A if way == 0 else B], ZH.at[q, way])
            else:
                arrived(i, ZF.at[q, way, step - 2])
                add_into(piece(m, j, dest), ZF.at[q, way, step - 2])
            z_copy(q, m, j, step, way).start()

    def z_sum(q, m, j):
        for way in range(2):
            arrived(ZR + 8 * q + 6 + way, ZF.at[q, way, 2])
        mine = piece(m, j, z)[...].astype(F32)
        return mine + ZF[q, 0, 2].astype(F32) + ZF[q, 1, 2].astype(F32)

    def z_end(q, m, j):
        total = z_sum(q, m, j)
        DM[m, p, j, zl] = total.astype(BF16)

    def s6(j):
        for n in (4, 7, 8, 9):
            ag_arrived(j, n)
        rows = R[j].reshape(1024, DC)
        down = lax.dot_general(HS[...], rows, (((0,), (0,)), ((), ())), preferred_element_type=F32)
        for e in range(4):
            for b in range(2):
                DM[2, e, j, b] = down[128 * e : 128 * (e + 1), DB * b : DB * (b + 1)].astype(BF16)
        z_start(j, 2, j)
        G[...] += lax.dot_general(
            rows, wd_cols(j), (((1,), (1,)), ((), ())), preferred_element_type=F32
        )

    stages = [s1, s2, s3, s4, s5, s6] + [
        functools.partial(lambda j, step: z_step(j, 2, j, step), step=step) for step in (1, 2, 3)
    ]

    late = {
        0: ((), (lambda: z3(7), lambda: z2(8))),
        1: ((), (lambda: z4(7), lambda: z3(8))),
        2: ((lambda: z5(7),), (lambda: z4(8),)),
        3: ((lambda: z5(8),), ()),
    }

    @pl.loop(0, 10)
    def _(t):
        for when, (before, _) in late.items():
            if before:

                @pl.when(t == when)
                def _():
                    for step in before:
                        step()

        @pl.when(t < 4)
        def _():
            s0(t)

        for when, (_, after) in late.items():
            if after:

                @pl.when(t == when)
                def _():
                    for step in after:
                        step()

        for n, stage in enumerate(stages):
            j = t - (n + 1)

            @pl.when((j >= 0) & (j < 4))
            def _():
                stage(j)

    sent(S_TOK, X.at[pl.ds(0, 7)])
    sent(S_W, DM.at[:, pl.ds(0, 3)])
    sent(S_META, FS.at[0, pl.ds(0, 8 * 22)])

    mean = jnp.sum(LS[...], axis=1, keepdims=True) * (0.5 / D)
    out[0, pl.ds(192, 1), pl.ds(0, TOK)] = jnp.sum(
        jnp.where(eye, mean, 0.0), axis=0, keepdims=True
    )

    @pl.loop(0, 8)
    def _(i):
        e, mb = i // 2, i % 2
        at = (pl.ds(pl.multiple_of(512 * mb, 512), 512), pl.ds(pl.multiple_of(128 * e, 128), 128))
        grad = G[at] * (column(mb, e) * column(mb, 4))
        pre = GU[e, mb]
        gate, up = pre[:, :128], pre[:, 128:]
        sig = jax.nn.sigmoid(gate)
        rows = at[0]
        GG[rows, pl.ds(pl.multiple_of(128 * e, 128), 128)] = (
            grad * up * (sig * (1.0 + gate * (1.0 - sig)))
        ).astype(BF16)
        GG[rows, pl.ds(pl.multiple_of(512 + 128 * e, 128), 128)] = (grad * (gate * sig)).astype(BF16)

    def dw_chunk(m, j):
        rows = X[:, :, dcols(j)].reshape(1024, DC)
        grads = lax.dot_general(
            GG[:, 512 * m : 512 * (m + 1)], rows, (((0,), (0,)), ((), ())),
            preferred_element_type=F32,
        )
        for e in range(4):
            for b in range(2):
                DM[m, e, j, b] = grads[128 * e : 128 * (e + 1), DB * b : DB * (b + 1)].astype(BF16)

    lo, hi = pl.ds(0, 2), pl.ds(2, 2)

    def yb_copy(n):
        src = (
            DM.at[0, lo, y2], DM.at[0, hi, y2], DM.at[0, hi, yu], DM.at[0, lo, yd],
            DM.at[0, lo, yu], DM.at[0, hi, yd],
        )[n]
        return rc(YB + n, src, YR1.at[n], y_up if n % 2 == 0 else y_dn, S_YB)

    def ys_copy(m, n):
        src = DM.at[m, p, (yu, yd, y2)[n], zl]
        dev = (y_up, y_dn, (y2 * 4 + zl * 2 + c, ex))[n]
        return rc(YS + 3 * (m - 1) + n, src, YR2.at[m - 1, n], dev, S_YS + m - 1)

    def yb_add(n, ref):
        arrived(YB + n, YR1.at[n])
        for a in range(2):
            for b in range(2):
                add_into(ref.at[a, b], YR1.at[n, a, b])

    def ys_start(m):
        for n in (2, 0, 1):
            ys_copy(m, n).start()

    def ys_sum(m):
        total = DM[m, p, y, zl].astype(F32)
        for n in (0, 1, 2):
            arrived(YS + 3 * (m - 1) + n, YR2.at[m - 1, n])
            total = total + YR2[m - 1, n].astype(F32)
        return total

    total_steps = jnp.sum(STEPS[...], axis=0)[4:5, :]
    mine_rows = pl.ds(pl.multiple_of(192 * c, 192), 192)
    other_rows = pl.ds(pl.multiple_of(192 * oc, 192), 192)

    def finish(m, total):
        FS[m] = total.T / total_steps
        rc(FX + m, FS.at[m, other_rows], FR.at[m], core, S_FX + m).start()

    def up_step(n, step):
        j = (y2, yu, yd, y)[n]
        if step == 0:
            z_start(4 + n, 1, j)
        elif step < 4:
            z_step(4 + n, 1, j, step)
        else:
            z_end(4 + n, 1, j)

    dw_chunk(0, y2)
    yb_copy(0).start()
    yb_copy(1).start()
    z_step(1, 2, 1, 3)
    z_step(2, 2, 2, 2)
    z_step(3, 2, 3, 1)
    dw_chunk(0, yu)
    yb_copy(2).start()
    dw_chunk(0, yd)
    yb_copy(3).start()
    dw_chunk(1, y2)
    up_step(0, 0)
    z_step(2, 2, 2, 3)
    z_step(3, 2, 3, 2)
    dw_chunk(1, yu)
    up_step(1, 0)
    dw_chunk(1, yd)
    up_step(2, 0)
    up_step(0, 1)
    z_step(3, 2, 3, 3)
    dw_chunk(1, y)
    up_step(3, 0)
    up_step(1, 1)
    yb_add(0, DM.at[0, lo, yu])
    yb_copy(4).start()
    yb_add(1, DM.at[0, hi, yd])
    yb_copy(5).start()
    up_step(0, 2)
    up_step(2, 1)
    dw_chunk(0, y)
    up_step(1, 2)
    up_step(3, 1)
    for j in range(4):
        z_end(j, 2, j)
    ys_start(2)
    up_step(0, 3)
    up_step(2, 2)
    up_step(1, 3)
    up_step(3, 2)
    yb_add(3, DM.at[0, lo, y])
    yb_add(2, DM.at[0, hi, y])
    up_step(2, 3)
    up_step(0, 4)
    up_step(3, 3)
    yb_add(4, DM.at[0, lo, y])
    yb_add(5, DM.at[0, hi, y])
    z_start(8, 0, y)
    up_step(1, 4)
    finish(2, ys_sum(2))
    up_step(2, 4)
    z_step(8, 0, y, 1)
    up_step(3, 4)
    ys_start(1)
    z_step(8, 0, y, 2)
    finish(1, ys_sum(1))
    z_step(8, 0, y, 3)
    finish(0, z_sum(8, 0, y))

    lanes = pl.ds(pl.multiple_of(128 * c, 128), 128)
    other_lanes = pl.ds(pl.multiple_of(128 * oc, 128), 128)
    for m in (2, 1, 0):
        out[m, pl.ds(0, 192), lanes] = FS[m, mine_rows]
        arrived(FX + m, FR.at[m])
        out[m, pl.ds(0, 192), other_lanes] = FR[m]

    for j in (2, 3):
        sent(S_PX + j, PSD.at[j % 2])
    sent(S_RX, DM.at[:, 0])
    sent(S_AG, X.at[pl.ds(0, 7)])
    for q in range(9):
        sent(S_ZR + q, W1.at[0, 0, pl.ds(0, 7 * 384)])
    sent(S_YB, DM.at[:, 0])
    for m in (1, 2):
        sent(S_YS + m - 1, YR2.at[m - 1])
    for m in range(3):
        sent(S_FX + m, FR.at[m])


def per_device(tokens, route_ids, route_mix, target, step_count, gate_weight, up_weight, down_weight):
    lines = jnp.arange(8, dtype=jnp.int32)[:, None, None]
    mix = jnp.sum(jnp.where(route_ids[None] == lines, route_mix[None], 0.0), axis=2)
    meta = jnp.where(lines[:, :, 0] == EXPERTS, step_count.astype(F32)[0], mix)
    any_spec = pl.BlockSpec(memory_space=pl.ANY)
    vmem_spec = pl.BlockSpec(memory_space=pltpu.VMEM)
    out = pl.pallas_call(
        kernel,
        out_shape=jax.ShapeDtypeStruct((3, 200, 256), F32),
        in_specs=[any_spec] * 6,
        out_specs=vmem_spec,
        scratch_shapes=[
            pltpu.VMEM((8, TOK, D), BF16),
            pltpu.VMEM((4, 2, D, 128), BF16),
            pltpu.VMEM((4, 128, D), BF16),
            pltpu.VMEM((4, 2, 512, 256), F32),
            pltpu.VMEM((1024, 512), BF16),
            pltpu.VMEM((1024, 512), BF16),
            pltpu.VMEM((8, TOK, 128), F32),
            pltpu.VMEM((8, 8, 128), F32),
            pltpu.VMEM((16, 8, 128), F32),
            pltpu.VMEM((4, 8, TOK, DC), BF16),
            pltpu.VMEM((2, 4, TOK, DC), BF16),
            pltpu.VMEM((4, 4, TOK, DC), BF16),
            pltpu.VMEM((4, 6, HALF, DC), BF16),
            pltpu.VMEM((TOK, D), BF16),
            pltpu.VMEM((1024, 512), F32),
            pltpu.VMEM((1024, 1024), BF16),
            pltpu.VMEM((3, 4, 4, 2, 128, DB), BF16),
            pltpu.VMEM((9, 2, HALF, DB), BF16),
            pltpu.VMEM((9, 2, 3, 128, DB), BF16),
            pltpu.VMEM((6, 2, 2, 128, DB), BF16),
            pltpu.VMEM((2, 3, 128, DB), BF16),
            pltpu.VMEM((3, DB, 128), F32),
            pltpu.VMEM((3, 192, 128), F32),
            pltpu.VMEM((TOK, 128), F32),
            pltpu.SemaphoreType.DMA((N_SEND,)),
            pltpu.SemaphoreType.DMA((N_SEM,)),
            pltpu.SemaphoreType.DMA((7,)),
        ],
        compiler_params=pltpu.CompilerParams(
            collective_id=0, has_side_effects=True, vmem_limit_bytes=67043328
        ),
    )(meta, tokens, target, gate_weight, up_weight, down_weight)
    return out[0, :192], out[1, :192], out[2, :192].T, out[0, 192, :TOK]


def solution(mesh):
    return jax.shard_map(
        per_device,
        mesh=mesh,
        in_specs=(
            P(("worker", "expert"), None),
            P(("worker", "expert"), None),
            P(("worker", "expert"), None),
            P(("worker", "expert"), None),
            P("worker"),
            P(None, "expert"),
            P(None, "expert"),
            P("expert", None),
        ),
        out_specs=(
            P("worker", "expert"),
            P("worker", "expert"),
            P("expert", "worker"),
            P(("worker", "expert")),
        ),
        check_vma=False,
    )
```

```python
import functools

import jax
import jax.numpy as jnp
from jax import lax
from jax.experimental import pallas as pl
from jax.experimental.pallas import tpu as pltpu
from jax.sharding import PartitionSpec as P

MESH = pl.DeviceIdType.MESH
F32 = jnp.float32
BF16 = jnp.bfloat16
EXPERTS = 4
TOK = 128
D = 3072
HALF = TOK // 2
DC = 768
DB = 384


class Ids:
    def __init__(self):
        self.n = 0

    def take(self, count):
        base = self.n
        self.n += count
        return base


IDS = Ids()
T_RA, T_RB, T_LA, T_LB, T_FR, T_FL, T_C, T_CL, T_CR, T_CF = (IDS.take(1) for _ in range(10))
MS = IDS.take(1)
Z1, Z2, Z3, Z4 = (IDS.take(9) for _ in range(4))
YQ = IDS.take(36)
PX = IDS.take(4)
RX = IDS.take(24)
AG = IDS.take(40)
ZR = IDS.take(80)
YB = IDS.take(12)
YS = IDS.take(6)
FX = IDS.take(3)
N_SEM = IDS.n
S_TOK, S_W, S_META, S_RX, S_AG, S_YB, S_YS, S_PX, S_ZR, N_SEND = 0, 1, 2, 3, 4, 5, 7, 9, 13, 23
S_FX = N_SEND
N_SEND += 3


def kernel(
    meta, tok, tgt, gw, uw, dw, out,
    X, W1, WD, GU, H, HS, MXB, META, STEPS, R, PSD, PRV, XR, G, GG, DM, ZH, ZF,
    YR1, YR2, YR3, FS, FR, LS, ssem, rsem, lsem,
):
    w = lax.axis_index("worker")
    ex = lax.axis_index("expert")
    y, zl, c = w // 4, (w // 2) % 2, w % 2
    p, x = ex // 4, ex % 4
    z = p * 2 + zl
    oc = 1 - c
    oz = 1 - zl
    xr, xl, x2 = (x + 1) % 4, (x + 3) % 4, (x + 2) % 4
    yu, yd, y2 = (y + 1) % 4, (y + 3) % 4, (y + 2) % 4
    e_out, e_in, e_opp = (p + 2 * zl + 3) % 4, (p + 5 - 2 * zl) % 4, (p + 2) % 4
    own = c * 4 + x
    right = (w, p * 4 + xr)
    left = (w, p * 4 + xl)
    core = (y * 4 + zl * 2 + oc, ex)
    z_out = (y * 4 + oz * 2 + c, e_out * 4 + x)
    z_in = (y * 4 + oz * 2 + c, ex)
    y_up = (yu * 4 + zl * 2 + c, ex)
    y_dn = (yd * 4 + zl * 2 + c, ex)
    zu, zd = (z + 1) % 8, (z + 7) % 8
    z_up = (y * 4 + (zu % 2) * 2 + c, (zu // 2) * 4 + x)
    z_dn = (y * 4 + (zd % 2) * 2 + c, (zd // 2) * 4 + x)

    def rc(i, src, dst, dev, group=0):
        return pltpu.make_async_remote_copy(
            src_ref=src, dst_ref=dst, send_sem=ssem.at[group], recv_sem=rsem.at[i],
            device_id=dev, device_id_type=MESH,
        )

    def send(i, src, dst, dev):
        rc(i, src, dst, dev, S_TOK if i < MS else S_W).start()

    def sent(group, ref):
        rc(0, ref, ref, core, group).wait_send()

    def arrived(i, dst):
        rc(i, dst, dst, core).wait_recv()

    loads = [
        pltpu.make_async_copy(gw.at[:, pl.ds(c * 128, 128)], W1.at[p, 0], lsem.at[0]),
        pltpu.make_async_copy(uw.at[:, pl.ds(c * 128, 128)], W1.at[p, 1], lsem.at[1]),
        pltpu.make_async_copy(dw.at[pl.ds(c * 128, 128)], WD.at[p], lsem.at[2]),
        pltpu.make_async_copy(tok, X.at[own], lsem.at[3]),
        pltpu.make_async_copy(meta, META.at[own], lsem.at[4]),
        pltpu.make_async_copy(meta, STEPS.at[w], lsem.at[5]),
    ] + [
        pltpu.make_async_copy(tgt.at[:, pl.ds(DC * j, DC)], R.at[j, own], lsem.at[6 + j])
        for j in range(4)
    ]
    for load in (loads[1], loads[0], loads[2], *loads[3:]):
        load.start()

    barrier = pltpu.get_barrier_semaphore()

    def greet(dev):
        pl.semaphore_signal(barrier, inc=1, device_id=dev, device_id_type=MESH)

    def slot_dev(s):
        return (y * 4 + zl * 2 + s // 4, p * 4 + s % 4)

    for i in range(1, 8):
        greet(slot_dev((own + i) % 8))
    for i in range(1, 16):
        other = (w + i) % 16
        greet((other, ex))
    greet(z_out)
    pl.semaphore_wait(barrier, 23)

    A, B = pl.ds(0, HALF), pl.ds(HALF, HALF)
    send(T_RA, tok.at[A], X.at[own, A], right)
    send(T_LB, tok.at[B], X.at[own, B], left)
    send(T_RB, tok.at[B], X.at[own, B], right)
    send(T_LA, tok.at[A], X.at[own, A], left)
    send(T_C, tok, X.at[own], core)

    quarter = {0: 768, 1: 256, 6: 32}
    along_y = (0, 1, 6)

    def rows_of(e, k, first, count):
        if k == 0:
            return W1.at[e, 1, pl.ds(first, count)]
        if k == 1:
            return W1.at[e, 0, pl.ds(2048 + first, count)]
        if k < 6:
            return W1.at[e, 0, pl.ds(512 * (k - 2) + first, count)]
        if k == 6:
            return WD.at[e, pl.ds(first, count), pl.ds(0, 1536)]
        return WD.at[e, pl.ds(first, count), pl.ds(1536 + 768 * (k - 7), 768)]

    def chunk(e, k, q):
        return rows_of(e, k, quarter[k] * q, quarter[k])

    def half(e, k, q, h):
        n = quarter[k] // 2
        return rows_of(e, k, quarter[k] * q + n * h, n)

    def zchunk(e, k):
        if k in quarter:
            return chunk(e, k, y)
        return rows_of(e, k, 0, 512 if k < 6 else 128)

    def zhalf(e, k, h):
        if k in quarter:
            return half(e, k, y, h)
        n = 256 if k < 6 else 64
        return rows_of(e, k, n * h, n)

    def z1(k):
        send(Z1 + k, zchunk(p, k), zchunk(p, k), z_out)

    def z2(k):
        arrived(Z1 + k, zchunk(e_out, k))
        send(Z2 + k, zchunk(e_out, k), zchunk(e_out, k), z_in)

    def z3(k):
        arrived(Z2 + k, zchunk(e_in, k))
        send(Z3 + k, zhalf(e_in, k, oz), zhalf(e_in, k, oz), z_out)

    def z4(k):
        arrived(Z3 + k, zhalf(e_opp, k, zl))
        send(Z4 + k, zhalf(e_opp, k, zl), zhalf(e_opp, k, zl), z_in)

    def z5(k):
        arrived(Z4 + k, zhalf(e_opp, k, oz))

    es = (e_out, e_in, e_opp)

    def yid(n, k):
        return YQ + (n * 3 + along_y.index(k)) * 4

    def yq(n, k):
        i = yid(n, k)
        send(i, chunk(es[n], k, y), chunk(es[n], k, y), y_up)
        send(i + 1, chunk(es[n], k, y), chunk(es[n], k, y), y_dn)

    def yf(n, k):
        i = yid(n, k)
        arrived(i, chunk(es[n], k, yd))
        send(i + 2, half(es[n], k, yd, 0), half(es[n], k, yd, 0), y_up)
        arrived(i + 1, chunk(es[n], k, yu))
        send(i + 3, half(es[n], k, yu, 1), half(es[n], k, yu, 1), y_dn)

    def ye(n, k):
        i = yid(n, k)
        arrived(i + 2, half(es[n], k, y2, 0))
        arrived(i + 3, half(es[n], k, y2, 1))

    lane4 = lax.broadcasted_iota(jnp.int32, (512, 128), 1)

    def column(mb, r):
        rows = MXB[pl.ds(4 * mb, 4)].reshape(512, 128)
        return jnp.sum(jnp.where(lane4 == r, rows, 0.0), axis=1, keepdims=True)

    def forward(e):
        @pl.loop(0, 2)
        def _(mb):
            rows = X[pl.ds(4 * mb, 4)].reshape(512, D)
            weights = jnp.concatenate([W1[e, 0], W1[e, 1]], axis=1)
            pre = jnp.dot(rows, weights, preferred_element_type=F32)
            GU[e, mb] = pre
            gate, up = pre[:, :128], pre[:, 128:]
            mixed = gate * jax.nn.sigmoid(gate) * up * column(mb, e)
            at = (
                pl.ds(pl.multiple_of(512 * mb, 512), 512),
                pl.ds(pl.multiple_of(128 * e, 128), 128),
            )
            H[at] = mixed.astype(BF16)
            HS[at] = (mixed * column(mb, 4)).astype(BF16)

    loads[1].wait()
    z1(0)
    loads[0].wait()
    z1(1)
    z1(2)
    z1(3)
    loads[2].wait()

    @pl.loop(1, 8)
    def _(i):
        rc(MS, meta, META.at[own], slot_dev((own + i) % 8), S_META).start()

    @pl.loop(1, 16)
    def _(i):
        rc(MS, meta, STEPS.at[w], ((w + i) % 16, ex), S_META).start()

    z2(0)
    yq(0, 0)
    z2(1)
    yq(0, 1)
    arrived(T_RA, X.at[c * 4 + xl, A])
    send(T_FR, X.at[c * 4 + xl, A], X.at[c * 4 + xl, A], right)
    arrived(T_LB, X.at[c * 4 + xr, B])
    send(T_FL, X.at[c * 4 + xr, B], X.at[c * 4 + xr, B], left)
    z2(2)
    z3(0)
    yq(1, 0)
    z3(1)
    yq(1, 1)
    z1(4)
    z1(5)
    z2(3)
    yf(0, 0)
    z3(2)
    z4(0)
    yf(0, 1)
    z4(1)
    z3(3)
    z1(6)
    arrived(T_RB, X.at[c * 4 + xl, B])
    send(T_CL, X.at[c * 4 + xl], X.at[c * 4 + xl], core)
    arrived(T_LA, X.at[c * 4 + xr, A])
    send(T_CR, X.at[c * 4 + xr], X.at[c * 4 + xr], core)
    z5(0)
    yq(2, 0)
    z5(1)
    yq(2, 1)
    z2(4)
    yf(1, 0)
    z2(5)
    z4(2)
    z3(4)
    yf(1, 1)
    z4(3)
    z3(5)
    z2(6)
    yq(0, 6)
    arrived(T_FR, X.at[c * 4 + x2, A])
    arrived(T_FL, X.at[c * 4 + x2, B])
    send(T_CF, X.at[c * 4 + x2], X.at[c * 4 + x2], core)

    for load in loads[3:]:
        load.wait()

    arrived(MS, FS.at[0, pl.ds(0, 8 * 22)])

    lane = lax.broadcasted_iota(jnp.int32, (TOK, 128), 1)
    eye = lane == lax.broadcasted_iota(jnp.int32, (TOK, 128), 0)

    @pl.loop(0, 8)
    def _(s):
        rows = META[s]
        cols = jnp.zeros((TOK, 128), F32)
        for r in range(5):
            spread = jnp.where(eye, jnp.broadcast_to(rows[r : r + 1, :], (TOK, 128)), 0.0)
            cols = cols + jnp.where(lane == r, jnp.sum(spread, axis=1, keepdims=True), 0.0)
        MXB[s] = cols

    z3(6)
    yq(1, 6)
    z1(7)
    z1(8)
    arrived(T_C, X.at[oc * 4 + x])
    arrived(T_CL, X.at[oc * 4 + xl])
    arrived(T_CR, X.at[oc * 4 + xr])
    arrived(T_CF, X.at[oc * 4 + x2])
    forward(p)
    yf(2, 0)
    z4(4)
    z4(5)
    z4(6)
    z5(6)
    yq(2, 6)
    yf(2, 1)
    ye(0, 0)
    ye(0, 1)
    forward(e_out)
    yf(0, 6)
    ye(1, 0)
    ye(1, 1)
    forward(e_in)
    yf(1, 6)
    for k in range(2, 6):
        z5(k)
    ye(2, 0)
    ye(2, 1)
    forward(e_opp)
    yf(2, 6)
    z2(7)
    for n in range(3):
        ye(n, 6)

    G[...] = jnp.zeros_like(G)
    LS[...] = jnp.zeros_like(LS)

    def dcols(j):
        return pl.ds(pl.multiple_of(DC * j, DC), DC)

    def wd_cols(j):
        return WD[:, :, dcols(j)].reshape(512, DC)

    def hrows(who):
        return H[pl.ds(pl.multiple_of(512 * who, 512), 512), :]

    def s0(j):
        slot = j % 2

        @pl.when(j >= 2)
        def _():
            sent(S_PX + j - 2, PSD.at[slot])

        part = jnp.dot(hrows(oc), wd_cols(j), preferred_element_type=F32)
        PSD[slot] = part.astype(BF16).reshape(4, TOK, DC)
        rc(PX + j, PSD.at[slot], PRV.at[j], core, S_PX + j).start()

    def rs_copy(j, n):
        src = (
            PRV.at[j, x2, A], PRV.at[j, x2, B], PRV.at[j, xr, B], PRV.at[j, xl, A],
            PRV.at[j, xr, A], PRV.at[j, xl, B],
        )[n]
        return rc(RX + 6 * j + n, src, XR.at[j, n], right if n % 2 == 0 else left, S_RX)

    def s1(j):
        arrived(PX + j, PRV.at[j])
        part = jnp.dot(hrows(c), wd_cols(j), preferred_element_type=F32)
        both = part.reshape(4, TOK, DC) + PRV[j].astype(F32)
        PRV[j] = both.astype(BF16)
        for n in range(4):
            rs_copy(j, n).start()

    def add_into(ref, other):
        ref[...] = ref[...] + other[...]

    def s2(j):
        arrived(RX + 6 * j, XR.at[j, 0])
        add_into(PRV.at[j, xr, A], XR.at[j, 0])
        rs_copy(j, 4).start()
        arrived(RX + 6 * j + 1, XR.at[j, 1])
        add_into(PRV.at[j, xl, B], XR.at[j, 1])
        rs_copy(j, 5).start()

    def ag_copy(j, n):
        i = AG + 10 * j + n
        if n < 4:
            h = (A, B, B, A)[n]
            return rc(i, R.at[j, own, h], R.at[j, own, h], (right, left)[n % 2], S_AG)
        if n == 4:
            return rc(i, R.at[j, own], R.at[j, own], core, S_AG)
        if n == 5:
            return rc(i, R.at[j, c * 4 + xl, A], R.at[j, c * 4 + xl, A], right, S_AG)
        if n == 6:
            return rc(i, R.at[j, c * 4 + xr, B], R.at[j, c * 4 + xr, B], left, S_AG)
        s = c * 4 + (xl, xr, x2)[n - 7]
        return rc(i, R.at[j, s], R.at[j, s], core, S_AG)

    def ag_arrived(j, n):
        i = AG + 10 * j + n
        near = c * 4 + (xl if n in (0, 2) else xr)
        far = oc * 4
        dst = {
            0: R.at[j, near, A], 2: R.at[j, near, B], 1: R.at[j, near, B], 3: R.at[j, near, A],
            4: R.at[j, far + x], 5: R.at[j, c * 4 + x2, A], 6: R.at[j, c * 4 + x2, B],
            7: R.at[j, far + xl], 8: R.at[j, far + xr], 9: R.at[j, far + x2],
        }[n]
        arrived(i, dst)

    def s3(j):
        for n in (2, 3, 4, 5):
            arrived(RX + 6 * j + n, XR.at[j, n])
        base = PRV[j, x].astype(F32)
        top = base[:HALF] + XR[j, 4].astype(F32) + XR[j, 3].astype(F32)
        low = base[HALF:] + XR[j, 2].astype(F32) + XR[j, 5].astype(F32)
        mixed = jnp.concatenate([top, low], axis=0)
        resid = mixed - R[j, own].astype(F32)
        square = resid * resid
        folded = square[:, :128]
        for n in range(1, 6):
            folded = folded + square[:, 128 * n : 128 * (n + 1)]
        LS[...] += folded
        R[j, own] = resid.astype(BF16)
        for n in (0, 1, 2, 3, 4):
            ag_copy(j, n).start()

    def s4(j):
        ag_arrived(j, 0)
        ag_copy(j, 5).start()
        ag_arrived(j, 1)
        ag_copy(j, 6).start()
        ag_arrived(j, 2)
        ag_copy(j, 7).start()
        ag_arrived(j, 3)
        ag_copy(j, 8).start()

    def s5(j):
        ag_arrived(j, 5)
        ag_arrived(j, 6)
        ag_copy(j, 9).start()

    def span(q):
        if isinstance(q, int) and 4 <= q < 8:
            return 0, 96
        return (96, 32) if isinstance(q, int) and q == 9 else (0, 128)

    def piece(q, m, j, dest):
        return DM.at[m, dest // 2, j, dest % 2, pl.ds(*span(q))]

    def side(q, way):
        count = span(q)[1] // 2
        return pl.ds(count * way, count)

    def zh(q, way):
        if isinstance(q, int) and q == 9:
            return ZH.at[4, way, pl.ds(48, 16)]
        return ZH.at[q, way, pl.ds(0, span(q)[1] // 2)]

    def zf(q, way, step):
        if isinstance(q, int) and q == 9:
            return ZF.at[4, way, step, pl.ds(96, 32)]
        return ZF.at[q, way, step, pl.ds(0, span(q)[1])]

    def z_copy(q, m, j, step, way):
        i = ZR + 8 * q + 2 * step + way
        dest = (z + (4 - step if way == 0 else 4 + step)) % 8
        dev = z_up if way == 0 else z_dn
        if step == 0:
            return rc(i, piece(q, m, j, dest).at[side(q, way)], zh(q, way), dev, S_ZR + q)
        return rc(i, piece(q, m, j, dest), zf(q, way, step - 1), dev, S_ZR + q)

    def z_start(q, m, j):
        z_copy(q, m, j, 0, 0).start()
        z_copy(q, m, j, 0, 1).start()

    def z_step(q, m, j, step):
        for way in range(2):
            i = ZR + 8 * q + 2 * (step - 1) + way
            dest = (z + (4 - step if way == 0 else 4 + step)) % 8
            if step == 1:
                arrived(i, zh(q, way))
                add_into(piece(q, m, j, dest).at[side(q, way)], zh(q, way))
            else:
                arrived(i, zf(q, way, step - 2))
                add_into(piece(q, m, j, dest), zf(q, way, step - 2))
            z_copy(q, m, j, step, way).start()

    def z_sum(q, m, j):
        for way in range(2):
            arrived(ZR + 8 * q + 6 + way, zf(q, way, 2))
        mine = piece(q, m, j, z)[...].astype(F32)
        return mine + zf(q, 0, 2)[...].astype(F32) + zf(q, 1, 2)[...].astype(F32)

    def z_end(q, m, j):
        total = z_sum(q, m, j)
        piece(q, m, j, z)[...] = total.astype(BF16)

    def s6(j):
        for n in (4, 7, 8, 9):
            ag_arrived(j, n)
        rows = R[j].reshape(1024, DC)
        down = lax.dot_general(HS[...], rows, (((0,), (0,)), ((), ())), preferred_element_type=F32)
        for e in range(4):
            for b in range(2):
                DM[2, e, j, b] = down[128 * e : 128 * (e + 1), DB * b : DB * (b + 1)].astype(BF16)
        z_start(j, 2, j)
        G[...] += lax.dot_general(
            rows, wd_cols(j), (((1,), (1,)), ((), ())), preferred_element_type=F32
        )

    stages = [s1, s2, s3, s4, s5, s6] + [
        functools.partial(lambda j, step: z_step(j, 2, j, step), step=step) for step in (1, 2, 3)
    ]

    late = {
        0: ((), (lambda: z3(7), lambda: z2(8))),
        1: ((), (lambda: z4(7), lambda: z3(8))),
        2: ((lambda: z5(7),), (lambda: z4(8),)),
        3: ((lambda: z5(8),), ()),
    }

    @pl.loop(0, 10)
    def _(t):
        for when, (before, _) in late.items():
            if before:

                @pl.when(t == when)
                def _():
                    for step in before:
                        step()

        @pl.when(t < 4)
        def _():
            s0(t)

        for when, (_, after) in late.items():
            if after:

                @pl.when(t == when)
                def _():
                    for step in after:
                        step()

        for n, stage in enumerate(stages):
            j = t - (n + 1)

            @pl.when((j >= 0) & (j < 4))
            def _():
                stage(j)

    sent(S_TOK, X.at[pl.ds(0, 7)])
    sent(S_W, DM.at[:, pl.ds(0, 3)])
    sent(S_META, FS.at[0, pl.ds(0, 8 * 22)])

    mean = jnp.sum(LS[...], axis=1, keepdims=True) * (0.5 / D)
    out[0, pl.ds(192, 1), pl.ds(0, TOK)] = jnp.sum(
        jnp.where(eye, mean, 0.0), axis=0, keepdims=True
    )

    @pl.loop(0, 8)
    def _(i):
        e, mb = i // 2, i % 2
        at = (pl.ds(pl.multiple_of(512 * mb, 512), 512), pl.ds(pl.multiple_of(128 * e, 128), 128))
        grad = G[at] * (column(mb, e) * column(mb, 4))
        pre = GU[e, mb]
        gate, up = pre[:, :128], pre[:, 128:]
        sig = jax.nn.sigmoid(gate)
        rows = at[0]
        GG[rows, pl.ds(pl.multiple_of(128 * e, 128), 128)] = (
            grad * up * (sig * (1.0 + gate * (1.0 - sig)))
        ).astype(BF16)
        GG[rows, pl.ds(pl.multiple_of(512 + 128 * e, 128), 128)] = (grad * (gate * sig)).astype(BF16)

    def dw_chunk(m, j):
        rows = X[:, :, dcols(j)].reshape(1024, DC)
        grads = lax.dot_general(
            GG[:, 512 * m : 512 * (m + 1)], rows, (((0,), (0,)), ((), ())),
            preferred_element_type=F32,
        )
        for e in range(4):
            for b in range(2):
                DM[m, e, j, b] = grads[128 * e : 128 * (e + 1), DB * b : DB * (b + 1)].astype(BF16)

    lo, hi = pl.ds(0, 2), pl.ds(2, 2)

    def yb_part(n, m):
        h = (lo, hi, hi, lo, lo, hi)[n]
        to = (y2, y2, yu, yd, yu, yd)[n]
        return yb_ref(h, to, m)

    def yb_ref(h, to, m):
        if m == 0:
            return DM.at[0, h, to]
        return DM.at[1, h, to, :, pl.ds(96, 32)]

    def yb_copy(n, m=0):
        dst = YR1.at[n] if m == 0 else YR3.at[n]
        return rc(YB + 6 * m + n, yb_part(n, m), dst, y_up if n % 2 == 0 else y_dn, S_YB + m)

    def ys_rows(m):
        return pl.ds(0, 96 if m == 1 else 128)

    def ys_copy(m, n):
        src = DM.at[m, p, (yu, yd, y2)[n], zl, ys_rows(m)]
        dev = (y_up, y_dn, (y2 * 4 + zl * 2 + c, ex))[n]
        return rc(YS + 3 * (m - 1) + n, src, YR2.at[m - 1, n, ys_rows(m)], dev, S_YS + m - 1)

    def yb_add(n, h, to, m=0):
        got = YR1 if m == 0 else YR3
        arrived(YB + 6 * m + n, got.at[n])
        ref = yb_ref(h, to, m)
        for a in range(2):
            for b in range(2):
                add_into(ref.at[a, b], got.at[n, a, b])

    def ys_start(m):
        for n in (2, 0, 1):
            ys_copy(m, n).start()

    def ys_sum(m):
        rows = ys_rows(m)
        total = DM[m, p, y, zl, rows].astype(F32)
        for n in (0, 1, 2):
            arrived(YS + 3 * (m - 1) + n, YR2.at[m - 1, n, rows])
            total = total + YR2[m - 1, n, rows].astype(F32)
        return total

    total_steps = jnp.sum(STEPS[...], axis=0)[4:5, :]
    mine_rows = pl.ds(pl.multiple_of(192 * c, 192), 192)
    other_rows = pl.ds(pl.multiple_of(192 * oc, 192), 192)

    def finish(m, total):
        FS[m] = total.T / total_steps
        rc(FX + m, FS.at[m, other_rows], FR.at[m], core, S_FX + m).start()

    def up_step(n, step):
        j = (y2, yu, yd, y)[n]
        if step == 0:
            z_start(4 + n, 1, j)
        elif step < 4:
            z_step(4 + n, 1, j, step)
        else:
            z_end(4 + n, 1, j)

    dw_chunk(0, y2)
    yb_copy(0).start()
    yb_copy(1).start()
    z_step(1, 2, 1, 3)
    z_step(2, 2, 2, 2)
    z_step(3, 2, 3, 1)
    dw_chunk(0, yu)
    yb_copy(2).start()
    dw_chunk(0, yd)
    yb_copy(3).start()
    dw_chunk(1, y2)
    yb_copy(0, 1).start()
    yb_copy(1, 1).start()
    up_step(0, 0)
    z_step(2, 2, 2, 3)
    z_step(3, 2, 3, 2)
    dw_chunk(1, yu)
    yb_copy(2, 1).start()
    up_step(1, 0)
    dw_chunk(1, yd)
    yb_copy(3, 1).start()
    up_step(2, 0)
    yb_add(0, lo, yu)
    yb_copy(4).start()
    yb_add(1, hi, yd)
    yb_copy(5).start()
    up_step(0, 1)
    z_step(3, 2, 3, 3)
    dw_chunk(1, y)
    up_step(3, 0)
    up_step(1, 1)
    dw_chunk(0, y)
    up_step(0, 2)
    up_step(2, 1)
    up_step(1, 2)
    up_step(3, 1)
    for j in range(4):
        z_end(j, 2, j)
    ys_start(2)
    yb_add(0, lo, yu, 1)
    yb_copy(4, 1).start()
    yb_add(1, hi, yd, 1)
    yb_copy(5, 1).start()
    up_step(0, 3)
    up_step(2, 2)
    up_step(1, 3)
    up_step(3, 2)
    yb_add(3, lo, y)
    yb_add(2, hi, y)
    yb_add(3, lo, y, 1)
    yb_add(2, hi, y, 1)
    up_step(2, 3)
    up_step(0, 4)
    yb_add(4, lo, y)
    yb_add(5, hi, y)
    z_start(8, 0, y)
    up_step(3, 3)
    up_step(1, 4)
    yb_add(4, lo, y, 1)
    yb_add(5, hi, y, 1)
    z_start(9, 1, y)
    z_step(8, 0, y, 1)
    up_step(2, 4)
    finish(2, ys_sum(2))
    z_step(9, 1, y, 1)
    z_step(8, 0, y, 2)
    up_step(3, 4)
    ys_start(1)
    z_step(9, 1, y, 2)
    z_step(8, 0, y, 3)
    z_step(9, 1, y, 3)
    finish(0, z_sum(8, 0, y))
    finish(1, jnp.concatenate([ys_sum(1), z_sum(9, 1, y)], axis=0))

    lanes = pl.ds(pl.multiple_of(128 * c, 128), 128)
    other_lanes = pl.ds(pl.multiple_of(128 * oc, 128), 128)
    for m in (2, 1, 0):
        out[m, pl.ds(0, 192), lanes] = FS[m, mine_rows]
        arrived(FX + m, FR.at[m])
        out[m, pl.ds(0, 192), other_lanes] = FR[m]

    for j in (2, 3):
        sent(S_PX + j, PSD.at[j % 2])
    sent(S_RX, DM.at[:, 0])
    sent(S_AG, X.at[pl.ds(0, 7)])
    for q in range(10):
        sent(S_ZR + q, W1.at[0, 0, pl.ds(0, 21 * span(q)[1])])
    sent(S_YB, DM.at[:, 0])
    sent(S_YB + 1, YR3)
    for m in (1, 2):
        sent(S_YS + m - 1, YR2.at[m - 1, :, ys_rows(m)])
    for m in range(3):
        sent(S_FX + m, FR.at[m])


def per_device(tokens, route_ids, route_mix, target, step_count, gate_weight, up_weight, down_weight):
    lines = jnp.arange(8, dtype=jnp.int32)[:, None, None]
    mix = jnp.sum(jnp.where(route_ids[None] == lines, route_mix[None], 0.0), axis=2)
    meta = jnp.where(lines[:, :, 0] == EXPERTS, step_count.astype(F32)[0], mix)
    any_spec = pl.BlockSpec(memory_space=pl.ANY)
    vmem_spec = pl.BlockSpec(memory_space=pltpu.VMEM)
    out = pl.pallas_call(
        kernel,
        out_shape=jax.ShapeDtypeStruct((3, 200, 256), F32),
        in_specs=[any_spec] * 6,
        out_specs=vmem_spec,
        scratch_shapes=[
            pltpu.VMEM((8, TOK, D), BF16),
            pltpu.VMEM((4, 2, D, 128), BF16),
            pltpu.VMEM((4, 128, D), BF16),
            pltpu.VMEM((4, 2, 512, 256), F32),
            pltpu.VMEM((1024, 512), BF16),
            pltpu.VMEM((1024, 512), BF16),
            pltpu.VMEM((8, TOK, 128), F32),
            pltpu.VMEM((8, 8, 128), F32),
            pltpu.VMEM((16, 8, 128), F32),
            pltpu.VMEM((4, 8, TOK, DC), BF16),
            pltpu.VMEM((2, 4, TOK, DC), BF16),
            pltpu.VMEM((4, 4, TOK, DC), BF16),
            pltpu.VMEM((4, 6, HALF, DC), BF16),
            pltpu.VMEM((1024, 512), F32),
            pltpu.VMEM((1024, 1024), BF16),
            pltpu.VMEM((3, 4, 4, 2, 128, DB), BF16),
            pltpu.VMEM((9, 2, HALF, DB), BF16),
            pltpu.VMEM((9, 2, 3, 128, DB), BF16),
            pltpu.VMEM((6, 2, 2, 128, DB), BF16),
            pltpu.VMEM((2, 3, 128, DB), BF16),
            pltpu.VMEM((6, 2, 2, 32, DB), BF16),
            pltpu.VMEM((3, DB, 128), F32),
            pltpu.VMEM((3, 192, 128), F32),
            pltpu.VMEM((TOK, 128), F32),
            pltpu.SemaphoreType.DMA((N_SEND,)),
            pltpu.SemaphoreType.DMA((N_SEM,)),
            pltpu.SemaphoreType.DMA((10,)),
        ],
        compiler_params=pltpu.CompilerParams(
            collective_id=0, has_side_effects=True, vmem_limit_bytes=67043328
        ),
    )(meta, tokens, target, gate_weight, up_weight, down_weight)
    return out[0, :192], out[1, :192], out[2, :192].T, out[0, 192, :TOK]


def solution(mesh):
    return jax.shard_map(
        per_device,
        mesh=mesh,
        in_specs=(
            P(("worker", "expert"), None),
            P(("worker", "expert"), None),
            P(("worker", "expert"), None),
            P(("worker", "expert"), None),
            P("worker"),
            P(None, "expert"),
            P(None, "expert"),
            P("expert", None),
        ),
        out_specs=(
            P("worker", "expert"),
            P("worker", "expert"),
            P("expert", "worker"),
            P(("worker", "expert")),
        ),
        check_vma=False,
    )
```

```python
import functools

import jax
import jax.numpy as jnp
from jax import lax
from jax.experimental import pallas as pl
from jax.experimental.pallas import tpu as pltpu
from jax.sharding import PartitionSpec as P

MESH = pl.DeviceIdType.MESH
F32 = jnp.float32
BF16 = jnp.bfloat16
EXPERTS = 4
TOK = 128
D = 3072
HALF = TOK // 2
DC = 768
DB = 384


class Ids:
    def __init__(self):
        self.n = 0

    def take(self, count):
        base = self.n
        self.n += count
        return base


IDS = Ids()
T_RA, T_RB, T_LA, T_LB, T_FR, T_FL, T_C, T_CL, T_CR, T_CF = (IDS.take(1) for _ in range(10))
MS = IDS.take(1)
Z1, Z2, Z3, Z4 = (IDS.take(9) for _ in range(4))
YQ = IDS.take(36)
PX = IDS.take(4)
RX = IDS.take(24)
AG = IDS.take(40)
ZR = IDS.take(80)
YB = IDS.take(12)
YS = IDS.take(6)
FX = IDS.take(3)
N_SEM = IDS.n
S_TOK, S_W, S_META, S_RX, S_AG, S_YB, S_YS, S_PX, S_ZR, N_SEND = 0, 1, 2, 3, 4, 5, 7, 9, 13, 23
S_FX = N_SEND
N_SEND += 3


def kernel(
    meta, tok, tgt, gw, uw, dw, out,
    X, W1, WD, GU, H, HS, MXB, META, STEPS, R, PSD, PRV, XR, G, GG, DM, ZH, ZF,
    YR1, YR2, YR3, FS, FR, LS, ssem, rsem, lsem,
):
    w = lax.axis_index("worker")
    ex = lax.axis_index("expert")
    y, zl, c = w // 4, (w // 2) % 2, w % 2
    p, x = ex // 4, ex % 4
    z = p * 2 + zl
    oc = 1 - c
    oz = 1 - zl
    xr, xl, x2 = (x + 1) % 4, (x + 3) % 4, (x + 2) % 4
    yu, yd, y2 = (y + 1) % 4, (y + 3) % 4, (y + 2) % 4
    e_out, e_in, e_opp = (p + 2 * zl + 3) % 4, (p + 5 - 2 * zl) % 4, (p + 2) % 4
    own = c * 4 + x
    right = (w, p * 4 + xr)
    left = (w, p * 4 + xl)
    core = (y * 4 + zl * 2 + oc, ex)
    z_out = (y * 4 + oz * 2 + c, e_out * 4 + x)
    z_in = (y * 4 + oz * 2 + c, ex)
    y_up = (yu * 4 + zl * 2 + c, ex)
    y_dn = (yd * 4 + zl * 2 + c, ex)
    zu, zd = (z + 1) % 8, (z + 7) % 8
    z_up = (y * 4 + (zu % 2) * 2 + c, (zu // 2) * 4 + x)
    z_dn = (y * 4 + (zd % 2) * 2 + c, (zd // 2) * 4 + x)

    def rc(i, src, dst, dev, group=0):
        return pltpu.make_async_remote_copy(
            src_ref=src, dst_ref=dst, send_sem=ssem.at[group], recv_sem=rsem.at[i],
            device_id=dev, device_id_type=MESH,
        )

    def send(i, src, dst, dev):
        rc(i, src, dst, dev, S_TOK if i < MS else S_W).start()

    def sent(group, ref):
        rc(0, ref, ref, core, group).wait_send()

    def arrived(i, dst):
        rc(i, dst, dst, core).wait_recv()

    loads = [
        pltpu.make_async_copy(gw.at[:, pl.ds(c * 128, 128)], W1.at[p, 0], lsem.at[0]),
        pltpu.make_async_copy(uw.at[:, pl.ds(c * 128, 128)], W1.at[p, 1], lsem.at[1]),
        pltpu.make_async_copy(dw.at[pl.ds(c * 128, 128)], WD.at[p], lsem.at[2]),
        pltpu.make_async_copy(tok, X.at[own], lsem.at[3]),
        pltpu.make_async_copy(meta, META.at[own], lsem.at[4]),
        pltpu.make_async_copy(meta, STEPS.at[w], lsem.at[5]),
    ] + [
        pltpu.make_async_copy(tgt.at[:, pl.ds(DC * j, DC)], R.at[j, own], lsem.at[6 + j])
        for j in range(4)
    ]
    for load in (loads[1], loads[0], loads[2], *loads[3:]):
        load.start()

    barrier = pltpu.get_barrier_semaphore()

    def greet(dev):
        pl.semaphore_signal(barrier, inc=1, device_id=dev, device_id_type=MESH)

    def slot_dev(s):
        return (y * 4 + zl * 2 + s // 4, p * 4 + s % 4)

    for i in range(1, 8):
        greet(slot_dev((own + i) % 8))
    for i in range(1, 16):
        other = (w + i) % 16
        greet((other, ex))
    greet(z_out)
    pl.semaphore_wait(barrier, 23)

    A, B = pl.ds(0, HALF), pl.ds(HALF, HALF)
    send(T_RA, tok.at[A], X.at[own, A], right)
    send(T_LB, tok.at[B], X.at[own, B], left)
    send(T_RB, tok.at[B], X.at[own, B], right)
    send(T_LA, tok.at[A], X.at[own, A], left)
    send(T_C, tok, X.at[own], core)

    quarter = {0: 768, 1: 256, 6: 32}
    along_y = (0, 1, 6)

    def rows_of(e, k, first, count):
        if k == 0:
            return W1.at[e, 1, pl.ds(first, count)]
        if k == 1:
            return W1.at[e, 0, pl.ds(2048 + first, count)]
        if k < 6:
            return W1.at[e, 0, pl.ds(512 * (k - 2) + first, count)]
        if k == 6:
            return WD.at[e, pl.ds(first, count), pl.ds(0, 1536)]
        return WD.at[e, pl.ds(first, count), pl.ds(1536 + 768 * (k - 7), 768)]

    def chunk(e, k, q):
        return rows_of(e, k, quarter[k] * q, quarter[k])

    def half(e, k, q, h):
        n = quarter[k] // 2
        return rows_of(e, k, quarter[k] * q + n * h, n)

    def zchunk(e, k):
        if k in quarter:
            return chunk(e, k, y)
        return rows_of(e, k, 0, 512 if k < 6 else 128)

    def zhalf(e, k, h):
        if k in quarter:
            return half(e, k, y, h)
        n = 256 if k < 6 else 64
        return rows_of(e, k, n * h, n)

    def z1(k):
        send(Z1 + k, zchunk(p, k), zchunk(p, k), z_out)

    def z2(k):
        arrived(Z1 + k, zchunk(e_out, k))
        send(Z2 + k, zchunk(e_out, k), zchunk(e_out, k), z_in)

    def z3(k):
        arrived(Z2 + k, zchunk(e_in, k))
        send(Z3 + k, zhalf(e_in, k, oz), zhalf(e_in, k, oz), z_out)

    def z4(k):
        arrived(Z3 + k, zhalf(e_opp, k, zl))
        send(Z4 + k, zhalf(e_opp, k, zl), zhalf(e_opp, k, zl), z_in)

    def z5(k):
        arrived(Z4 + k, zhalf(e_opp, k, oz))

    es = (e_out, e_in, e_opp)

    def yid(n, k):
        return YQ + (n * 3 + along_y.index(k)) * 4

    def yq(n, k):
        i = yid(n, k)
        send(i, chunk(es[n], k, y), chunk(es[n], k, y), y_up)
        send(i + 1, chunk(es[n], k, y), chunk(es[n], k, y), y_dn)

    def yf(n, k):
        i = yid(n, k)
        arrived(i, chunk(es[n], k, yd))
        send(i + 2, half(es[n], k, yd, 0), half(es[n], k, yd, 0), y_up)
        arrived(i + 1, chunk(es[n], k, yu))
        send(i + 3, half(es[n], k, yu, 1), half(es[n], k, yu, 1), y_dn)

    def ye(n, k):
        i = yid(n, k)
        arrived(i + 2, half(es[n], k, y2, 0))
        arrived(i + 3, half(es[n], k, y2, 1))

    lane4 = lax.broadcasted_iota(jnp.int32, (512, 128), 1)

    def column(mb, r):
        rows = MXB[pl.ds(4 * mb, 4)].reshape(512, 128)
        return jnp.sum(jnp.where(lane4 == r, rows, 0.0), axis=1, keepdims=True)

    def forward(e):
        @pl.loop(0, 2)
        def _(mb):
            rows = X[pl.ds(4 * mb, 4)].reshape(512, D)
            weights = jnp.concatenate([W1[e, 0], W1[e, 1]], axis=1)
            pre = jnp.dot(rows, weights, preferred_element_type=F32)
            GU[e, mb] = pre
            gate, up = pre[:, :128], pre[:, 128:]
            mixed = gate * jax.nn.sigmoid(gate) * up * column(mb, e)
            at = (
                pl.ds(pl.multiple_of(512 * mb, 512), 512),
                pl.ds(pl.multiple_of(128 * e, 128), 128),
            )
            H[at] = mixed.astype(BF16)
            HS[at] = (mixed * column(mb, 4)).astype(BF16)

    loads[1].wait()
    z1(0)
    loads[0].wait()
    z1(1)
    z1(2)
    z1(3)
    loads[2].wait()

    @pl.loop(1, 8)
    def _(i):
        rc(MS, meta, META.at[own], slot_dev((own + i) % 8), S_META).start()

    @pl.loop(1, 16)
    def _(i):
        rc(MS, meta, STEPS.at[w], ((w + i) % 16, ex), S_META).start()

    z2(0)
    yq(0, 0)
    z2(1)
    yq(0, 1)
    arrived(T_RA, X.at[c * 4 + xl, A])
    send(T_FR, X.at[c * 4 + xl, A], X.at[c * 4 + xl, A], right)
    arrived(T_LB, X.at[c * 4 + xr, B])
    send(T_FL, X.at[c * 4 + xr, B], X.at[c * 4 + xr, B], left)
    z2(2)
    z3(0)
    yq(1, 0)
    z3(1)
    yq(1, 1)
    z1(4)
    z1(5)
    z2(3)
    yf(0, 0)
    z3(2)
    z4(0)
    yf(0, 1)
    z4(1)
    z3(3)
    z1(6)
    arrived(T_RB, X.at[c * 4 + xl, B])
    send(T_CL, X.at[c * 4 + xl], X.at[c * 4 + xl], core)
    arrived(T_LA, X.at[c * 4 + xr, A])
    send(T_CR, X.at[c * 4 + xr], X.at[c * 4 + xr], core)
    z5(0)
    yq(2, 0)
    z5(1)
    yq(2, 1)
    z2(4)
    yf(1, 0)
    z2(5)
    z4(2)
    z3(4)
    yf(1, 1)
    z4(3)
    z3(5)
    z2(6)
    yq(0, 6)
    arrived(T_FR, X.at[c * 4 + x2, A])
    arrived(T_FL, X.at[c * 4 + x2, B])
    send(T_CF, X.at[c * 4 + x2], X.at[c * 4 + x2], core)

    for load in loads[3:]:
        load.wait()

    arrived(MS, FS.at[0, pl.ds(0, 8 * 22)])

    lane = lax.broadcasted_iota(jnp.int32, (TOK, 128), 1)
    eye = lane == lax.broadcasted_iota(jnp.int32, (TOK, 128), 0)

    @pl.loop(0, 8)
    def _(s):
        rows = META[s]
        cols = jnp.zeros((TOK, 128), F32)
        for r in range(5):
            spread = jnp.where(eye, jnp.broadcast_to(rows[r : r + 1, :], (TOK, 128)), 0.0)
            cols = cols + jnp.where(lane == r, jnp.sum(spread, axis=1, keepdims=True), 0.0)
        MXB[s] = cols

    z3(6)
    yq(1, 6)
    z1(7)
    z1(8)
    arrived(T_C, X.at[oc * 4 + x])
    arrived(T_CL, X.at[oc * 4 + xl])
    arrived(T_CR, X.at[oc * 4 + xr])
    arrived(T_CF, X.at[oc * 4 + x2])
    forward(p)
    yf(2, 0)
    z4(4)
    z4(5)
    z4(6)
    z5(6)
    yq(2, 6)
    yf(2, 1)
    ye(0, 0)
    ye(0, 1)
    forward(e_out)
    yf(0, 6)
    ye(1, 0)
    ye(1, 1)
    forward(e_in)
    yf(1, 6)
    for k in range(2, 6):
        z5(k)
    ye(2, 0)
    ye(2, 1)
    forward(e_opp)
    yf(2, 6)
    z2(7)
    for n in range(3):
        ye(n, 6)

    G[...] = jnp.zeros_like(G)
    LS[...] = jnp.zeros_like(LS)

    def dcols(j):
        return pl.ds(pl.multiple_of(DC * j, DC), DC)

    def wd_cols(j):
        return WD[:, :, dcols(j)].reshape(512, DC)

    def hrows(who):
        return H[pl.ds(pl.multiple_of(512 * who, 512), 512), :]

    def s0(j):
        slot = j % 2

        @pl.when(j >= 2)
        def _():
            sent(S_PX + j - 2, PSD.at[slot])

        part = jnp.dot(hrows(oc), wd_cols(j), preferred_element_type=F32)
        PSD[slot] = part.astype(BF16).reshape(4, TOK, DC)
        rc(PX + j, PSD.at[slot], PRV.at[j], core, S_PX + j).start()

    def rs_copy(j, n):
        src = (
            PRV.at[j, x2, A], PRV.at[j, x2, B], PRV.at[j, xr, B], PRV.at[j, xl, A],
            PRV.at[j, xr, A], PRV.at[j, xl, B],
        )[n]
        return rc(RX + 6 * j + n, src, XR.at[j, n], right if n % 2 == 0 else left, S_RX)

    def s1(j):
        arrived(PX + j, PRV.at[j])
        part = jnp.dot(hrows(c), wd_cols(j), preferred_element_type=F32)
        both = part.reshape(4, TOK, DC) + PRV[j].astype(F32)
        PRV[j] = both.astype(BF16)
        for n in range(4):
            rs_copy(j, n).start()

    def add_into(ref, other):
        ref[...] = ref[...] + other[...]

    def s2(j):
        arrived(RX + 6 * j, XR.at[j, 0])
        add_into(PRV.at[j, xr, A], XR.at[j, 0])
        rs_copy(j, 4).start()
        arrived(RX + 6 * j + 1, XR.at[j, 1])
        add_into(PRV.at[j, xl, B], XR.at[j, 1])
        rs_copy(j, 5).start()

    def ag_copy(j, n):
        i = AG + 10 * j + n
        if n < 4:
            h = (A, B, B, A)[n]
            return rc(i, R.at[j, own, h], R.at[j, own, h], (right, left)[n % 2], S_AG)
        if n == 4:
            return rc(i, R.at[j, own], R.at[j, own], core, S_AG)
        if n == 5:
            return rc(i, R.at[j, c * 4 + xl, A], R.at[j, c * 4 + xl, A], right, S_AG)
        if n == 6:
            return rc(i, R.at[j, c * 4 + xr, B], R.at[j, c * 4 + xr, B], left, S_AG)
        s = c * 4 + (xl, xr, x2)[n - 7]
        return rc(i, R.at[j, s], R.at[j, s], core, S_AG)

    def ag_arrived(j, n):
        i = AG + 10 * j + n
        near = c * 4 + (xl if n in (0, 2) else xr)
        far = oc * 4
        dst = {
            0: R.at[j, near, A], 2: R.at[j, near, B], 1: R.at[j, near, B], 3: R.at[j, near, A],
            4: R.at[j, far + x], 5: R.at[j, c * 4 + x2, A], 6: R.at[j, c * 4 + x2, B],
            7: R.at[j, far + xl], 8: R.at[j, far + xr], 9: R.at[j, far + x2],
        }[n]
        arrived(i, dst)

    def s3(j):
        for n in (2, 3, 4, 5):
            arrived(RX + 6 * j + n, XR.at[j, n])
        base = PRV[j, x].astype(F32)
        top = base[:HALF] + XR[j, 4].astype(F32) + XR[j, 3].astype(F32)
        low = base[HALF:] + XR[j, 2].astype(F32) + XR[j, 5].astype(F32)
        mixed = jnp.concatenate([top, low], axis=0)
        resid = mixed - R[j, own].astype(F32)
        square = resid * resid
        folded = square[:, :128]
        for n in range(1, 6):
            folded = folded + square[:, 128 * n : 128 * (n + 1)]
        LS[...] += folded
        R[j, own] = resid.astype(BF16)
        for n in (0, 1, 2, 3, 4):
            ag_copy(j, n).start()

    def s4(j):
        ag_arrived(j, 0)
        ag_copy(j, 5).start()
        ag_arrived(j, 1)
        ag_copy(j, 6).start()
        ag_arrived(j, 2)
        ag_copy(j, 7).start()
        ag_arrived(j, 3)
        ag_copy(j, 8).start()

    def s5(j):
        ag_arrived(j, 5)
        ag_arrived(j, 6)
        ag_copy(j, 9).start()

    def span(q):
        if isinstance(q, int) and 4 <= q < 8:
            return 0, 96
        return (96, 32) if isinstance(q, int) and q == 9 else (0, 128)

    def piece(q, m, j, dest):
        return DM.at[m, dest // 2, j, dest % 2, pl.ds(*span(q))]

    def side(q, way):
        count = span(q)[1] // 2
        return pl.ds(count * way, count)

    def zh(q, way):
        if isinstance(q, int) and q == 9:
            return ZH.at[4, way, pl.ds(48, 16)]
        return ZH.at[q, way, pl.ds(0, span(q)[1] // 2)]

    def zf(q, way, step):
        if isinstance(q, int) and q == 9:
            return ZF.at[4, way, step, pl.ds(96, 32)]
        return ZF.at[q, way, step, pl.ds(0, span(q)[1])]

    def z_copy(q, m, j, step, way):
        i = ZR + 8 * q + 2 * step + way
        dest = (z + (4 - step if way == 0 else 4 + step)) % 8
        dev = z_up if way == 0 else z_dn
        if step == 0:
            return rc(i, piece(q, m, j, dest).at[side(q, way)], zh(q, way), dev, S_ZR + q)
        return rc(i, piece(q, m, j, dest), zf(q, way, step - 1), dev, S_ZR + q)

    def z_start(q, m, j):
        z_copy(q, m, j, 0, 0).start()
        z_copy(q, m, j, 0, 1).start()

    def z_step(q, m, j, step):
        for way in range(2):
            i = ZR + 8 * q + 2 * (step - 1) + way
            dest = (z + (4 - step if way == 0 else 4 + step)) % 8
            if step == 1:
                arrived(i, zh(q, way))
                add_into(piece(q, m, j, dest).at[side(q, way)], zh(q, way))
            else:
                arrived(i, zf(q, way, step - 2))
                add_into(piece(q, m, j, dest), zf(q, way, step - 2))
            z_copy(q, m, j, step, way).start()

    def z_sum(q, m, j):
        for way in range(2):
            arrived(ZR + 8 * q + 6 + way, zf(q, way, 2))
        mine = piece(q, m, j, z)[...].astype(F32)
        return mine + zf(q, 0, 2)[...].astype(F32) + zf(q, 1, 2)[...].astype(F32)

    def z_end(q, m, j):
        total = z_sum(q, m, j)
        piece(q, m, j, z)[...] = total.astype(BF16)

    def s6(j):
        for n in (4, 7, 8, 9):
            ag_arrived(j, n)
        rows = R[j].reshape(1024, DC)
        down = lax.dot_general(HS[...], rows, (((0,), (0,)), ((), ())), preferred_element_type=F32)
        for e in range(4):
            for b in range(2):
                DM[2, e, j, b] = down[128 * e : 128 * (e + 1), DB * b : DB * (b + 1)].astype(BF16)
        z_start(j, 2, j)
        G[...] += lax.dot_general(
            rows, wd_cols(j), (((1,), (1,)), ((), ())), preferred_element_type=F32
        )

    stages = [s1, s2, s3, s4, s5, s6] + [
        functools.partial(lambda j, step: z_step(j, 2, j, step), step=step) for step in (1, 2, 3)
    ]

    late = {
        0: ((), (lambda: z3(7), lambda: z2(8))),
        1: ((), (lambda: z4(7), lambda: z3(8))),
        2: ((lambda: z5(7),), (lambda: z4(8),)),
        3: ((lambda: z5(8),), ()),
    }

    @pl.loop(0, 10)
    def _(t):
        for when, (before, _) in late.items():
            if before:

                @pl.when(t == when)
                def _():
                    for step in before:
                        step()

        @pl.when(t < 4)
        def _():
            s0(t)

        for when, (_, after) in late.items():
            if after:

                @pl.when(t == when)
                def _():
                    for step in after:
                        step()

        for n in (1, 2, 3, 4, 0, 5, 6, 7, 8):
            stage = stages[n]
            j = t - (n + 1)

            @pl.when((j >= 0) & (j < 4))
            def _():
                stage(j)

    sent(S_TOK, X.at[pl.ds(0, 7)])
    sent(S_W, DM.at[:, pl.ds(0, 3)])
    sent(S_META, FS.at[0, pl.ds(0, 8 * 22)])

    mean = jnp.sum(LS[...], axis=1, keepdims=True) * (0.5 / D)
    out[0, pl.ds(192, 1), pl.ds(0, TOK)] = jnp.sum(
        jnp.where(eye, mean, 0.0), axis=0, keepdims=True
    )

    @pl.loop(0, 8)
    def _(i):
        e, mb = i // 2, i % 2
        at = (pl.ds(pl.multiple_of(512 * mb, 512), 512), pl.ds(pl.multiple_of(128 * e, 128), 128))
        grad = G[at] * (column(mb, e) * column(mb, 4))
        pre = GU[e, mb]
        gate, up = pre[:, :128], pre[:, 128:]
        sig = jax.nn.sigmoid(gate)
        rows = at[0]
        GG[rows, pl.ds(pl.multiple_of(128 * e, 128), 128)] = (
            grad * up * (sig * (1.0 + gate * (1.0 - sig)))
        ).astype(BF16)
        GG[rows, pl.ds(pl.multiple_of(512 + 128 * e, 128), 128)] = (grad * (gate * sig)).astype(BF16)

    def dw_chunk(m, j):
        rows = X[:, :, dcols(j)].reshape(1024, DC)
        grads = lax.dot_general(
            GG[:, 512 * m : 512 * (m + 1)], rows, (((0,), (0,)), ((), ())),
            preferred_element_type=F32,
        )
        for e in range(4):
            for b in range(2):
                DM[m, e, j, b] = grads[128 * e : 128 * (e + 1), DB * b : DB * (b + 1)].astype(BF16)

    lo, hi = pl.ds(0, 2), pl.ds(2, 2)

    def yb_part(n, m):
        h = (lo, hi, hi, lo, lo, hi)[n]
        to = (y2, y2, yu, yd, yu, yd)[n]
        return yb_ref(h, to, m)

    def yb_ref(h, to, m):
        if m == 0:
            return DM.at[0, h, to]
        return DM.at[1, h, to, :, pl.ds(96, 32)]

    def yb_copy(n, m=0):
        dst = YR1.at[n] if m == 0 else YR3.at[n]
        return rc(YB + 6 * m + n, yb_part(n, m), dst, y_up if n % 2 == 0 else y_dn, S_YB + m)

    def ys_rows(m):
        return pl.ds(0, 96 if m == 1 else 128)

    def ys_copy(m, n):
        src = DM.at[m, p, (yu, yd, y2)[n], zl, ys_rows(m)]
        dev = (y_up, y_dn, (y2 * 4 + zl * 2 + c, ex))[n]
        return rc(YS + 3 * (m - 1) + n, src, YR2.at[m - 1, n, ys_rows(m)], dev, S_YS + m - 1)

    def yb_add(n, h, to, m=0):
        got = YR1 if m == 0 else YR3
        arrived(YB + 6 * m + n, got.at[n])
        ref = yb_ref(h, to, m)
        for a in range(2):
            for b in range(2):
                add_into(ref.at[a, b], got.at[n, a, b])

    def ys_start(m):
        for n in (2, 0, 1):
            ys_copy(m, n).start()

    def ys_sum(m):
        rows = ys_rows(m)
        total = DM[m, p, y, zl, rows].astype(F32)
        for n in (0, 1, 2):
            arrived(YS + 3 * (m - 1) + n, YR2.at[m - 1, n, rows])
            total = total + YR2[m - 1, n, rows].astype(F32)
        return total

    total_steps = jnp.sum(STEPS[...], axis=0)[4:5, :]
    mine_rows = pl.ds(pl.multiple_of(192 * c, 192), 192)
    other_rows = pl.ds(pl.multiple_of(192 * oc, 192), 192)

    def finish(m, total):
        FS[m] = total.T / total_steps
        rc(FX + m, FS.at[m, other_rows], FR.at[m], core, S_FX + m).start()

    def up_step(n, step):
        j = (y2, yu, yd, y)[n]
        if step == 0:
            z_start(4 + n, 1, j)
        elif step < 4:
            z_step(4 + n, 1, j, step)
        else:
            z_end(4 + n, 1, j)

    dw_chunk(0, y2)
    yb_copy(0).start()
    yb_copy(1).start()
    z_step(1, 2, 1, 3)
    z_step(2, 2, 2, 2)
    z_step(3, 2, 3, 1)
    dw_chunk(0, yu)
    yb_copy(2).start()
    dw_chunk(0, yd)
    yb_copy(3).start()
    dw_chunk(1, y2)
    yb_copy(0, 1).start()
    yb_copy(1, 1).start()
    up_step(0, 0)
    z_step(2, 2, 2, 3)
    z_step(3, 2, 3, 2)
    dw_chunk(1, yu)
    yb_copy(2, 1).start()
    up_step(1, 0)
    dw_chunk(1, yd)
    yb_copy(3, 1).start()
    up_step(2, 0)
    yb_add(0, lo, yu)
    yb_copy(4).start()
    yb_add(1, hi, yd)
    yb_copy(5).start()
    up_step(0, 1)
    z_step(3, 2, 3, 3)
    dw_chunk(1, y)
    up_step(3, 0)
    up_step(1, 1)
    dw_chunk(0, y)
    up_step(0, 2)
    up_step(2, 1)
    up_step(1, 2)
    up_step(3, 1)
    for j in range(4):
        z_end(j, 2, j)
    ys_start(2)
    yb_add(0, lo, yu, 1)
    yb_copy(4, 1).start()
    yb_add(1, hi, yd, 1)
    yb_copy(5, 1).start()
    up_step(0, 3)
    up_step(2, 2)
    up_step(1, 3)
    up_step(3, 2)
    yb_add(3, lo, y)
    yb_add(2, hi, y)
    yb_add(3, lo, y, 1)
    yb_add(2, hi, y, 1)
    up_step(2, 3)
    up_step(0, 4)
    yb_add(4, lo, y)
    yb_add(5, hi, y)
    z_start(8, 0, y)
    up_step(3, 3)
    up_step(1, 4)
    yb_add(4, lo, y, 1)
    yb_add(5, hi, y, 1)
    z_start(9, 1, y)
    z_step(8, 0, y, 1)
    up_step(2, 4)
    finish(2, ys_sum(2))
    z_step(9, 1, y, 1)
    z_step(8, 0, y, 2)
    up_step(3, 4)
    ys_start(1)
    z_step(9, 1, y, 2)
    z_step(8, 0, y, 3)
    z_step(9, 1, y, 3)
    finish(0, z_sum(8, 0, y))
    finish(1, jnp.concatenate([ys_sum(1), z_sum(9, 1, y)], axis=0))

    lanes = pl.ds(pl.multiple_of(128 * c, 128), 128)
    other_lanes = pl.ds(pl.multiple_of(128 * oc, 128), 128)
    for m in (2, 1, 0):
        out[m, pl.ds(0, 192), lanes] = FS[m, mine_rows]
        arrived(FX + m, FR.at[m])
        out[m, pl.ds(0, 192), other_lanes] = FR[m]

    for j in (2, 3):
        sent(S_PX + j, PSD.at[j % 2])
    sent(S_RX, DM.at[:, 0])
    sent(S_AG, X.at[pl.ds(0, 7)])
    for q in range(10):
        sent(S_ZR + q, W1.at[0, 0, pl.ds(0, 21 * span(q)[1])])
    sent(S_YB, DM.at[:, 0])
    sent(S_YB + 1, YR3)
    for m in (1, 2):
        sent(S_YS + m - 1, YR2.at[m - 1, :, ys_rows(m)])
    for m in range(3):
        sent(S_FX + m, FR.at[m])


def per_device(tokens, route_ids, route_mix, target, step_count, gate_weight, up_weight, down_weight):
    lines = jnp.arange(8, dtype=jnp.int32)[:, None, None]
    mix = jnp.sum(jnp.where(route_ids[None] == lines, route_mix[None], 0.0), axis=2)
    meta = jnp.where(lines[:, :, 0] == EXPERTS, step_count.astype(F32)[0], mix)
    any_spec = pl.BlockSpec(memory_space=pl.ANY)
    vmem_spec = pl.BlockSpec(memory_space=pltpu.VMEM)
    out = pl.pallas_call(
        kernel,
        out_shape=jax.ShapeDtypeStruct((3, 200, 256), F32),
        in_specs=[any_spec] * 6,
        out_specs=vmem_spec,
        scratch_shapes=[
            pltpu.VMEM((8, TOK, D), BF16),
            pltpu.VMEM((4, 2, D, 128), BF16),
            pltpu.VMEM((4, 128, D), BF16),
            pltpu.VMEM((4, 2, 512, 256), F32),
            pltpu.VMEM((1024, 512), BF16),
            pltpu.VMEM((1024, 512), BF16),
            pltpu.VMEM((8, TOK, 128), F32),
            pltpu.VMEM((8, 8, 128), F32),
            pltpu.VMEM((16, 8, 128), F32),
            pltpu.VMEM((4, 8, TOK, DC), BF16),
            pltpu.VMEM((2, 4, TOK, DC), BF16),
            pltpu.VMEM((4, 4, TOK, DC), BF16),
            pltpu.VMEM((4, 6, HALF, DC), BF16),
            pltpu.VMEM((1024, 512), F32),
            pltpu.VMEM((1024, 1024), BF16),
            pltpu.VMEM((3, 4, 4, 2, 128, DB), BF16),
            pltpu.VMEM((9, 2, HALF, DB), BF16),
            pltpu.VMEM((9, 2, 3, 128, DB), BF16),
            pltpu.VMEM((6, 2, 2, 128, DB), BF16),
            pltpu.VMEM((2, 3, 128, DB), BF16),
            pltpu.VMEM((6, 2, 2, 32, DB), BF16),
            pltpu.VMEM((3, DB, 128), F32),
            pltpu.VMEM((3, 192, 128), F32),
            pltpu.VMEM((TOK, 128), F32),
            pltpu.SemaphoreType.DMA((N_SEND,)),
            pltpu.SemaphoreType.DMA((N_SEM,)),
            pltpu.SemaphoreType.DMA((10,)),
        ],
        compiler_params=pltpu.CompilerParams(
            collective_id=0, has_side_effects=True, vmem_limit_bytes=67043328
        ),
    )(meta, tokens, target, gate_weight, up_weight, down_weight)
    return out[0, :192], out[1, :192], out[2, :192].T, out[0, 192, :TOK]


def solution(mesh):
    return jax.shard_map(
        per_device,
        mesh=mesh,
        in_specs=(
            P(("worker", "expert"), None),
            P(("worker", "expert"), None),
            P(("worker", "expert"), None),
            P(("worker", "expert"), None),
            P("worker"),
            P(None, "expert"),
            P(None, "expert"),
            P("expert", None),
        ),
        out_specs=(
            P("worker", "expert"),
            P("worker", "expert"),
            P("expert", "worker"),
            P(("worker", "expert")),
        ),
        check_vma=False,
    )
```
